512 devices in a mesh: phase: 8 (over x, core), expert: 64 (over y, z).
Axes of the slice: x: 4, y: 8, z: 8, core: 2. Of those that a mesh axis runs over, the one named last changes fastest.
Arguments:
- fwd_acts: bfloat16 [8, 8192, 2048], P('phase', 'expert'), may hold values from -6 to 6
- fwd_routes: int32 [8, 8192, 1], P('phase', 'expert'), may hold values from 0 to 7; in each aligned block of 128 rows (0 to 127, 128 to 255, ..., all dimensions but the last counted through in order) at most 18 rows name the same one
- fwd_weights: float32 [8, 8192, 1], P('phase', 'expert'), may hold values from 0.1 to 1
- fwd_lengths: int32 [8, 16], P('phase'), may hold values from 1 to 2048, 8192 in all within a row
- fwd_tenants: int32 [8, 16], P('phase'), may hold values from 0 to 1
- bwd_acts: bfloat16 [8, 8192, 2048], P('phase', 'expert'), may hold values from -6 to 6
- bwd_routes: int32 [8, 8192, 1], P('phase', 'expert'), may hold values from 0 to 7; in each aligned block of 128 rows (0 to 127, 128 to 255, ..., all dimensions but the last counted through in order) at most 18 rows name the same one
- bwd_weights: float32 [8, 8192, 1], P('phase', 'expert'), may hold values from 0.1 to 1
- bwd_lengths: int32 [8, 16], P('phase'), may hold values from 1 to 2048, 8192 in all within a row
- bwd_tenants: int32 [8, 16], P('phase'), may hold values from 0 to 1
- bwd_cotangent: bfloat16 [8, 8192, 2048], P('phase', 'expert'), may hold values from -6 to 6
- prompts: bfloat16 [8, 2, 10, 2048], P('phase'), may hold values from -6 to 6
- norm_gain: float32 [8, 2048], P('phase'), may hold values from 0.1 to 1.9
- w_gate: bfloat16 [8, 64, 2048, 128], P('phase', 'expert'), may hold values from -0.125 to 0.125
- w_up: bfloat16 [8, 64, 2048, 128], P('phase', 'expert'), may hold values from -0.125 to 0.125
- w_down: bfloat16 [8, 64, 128, 2048], P('phase', 'expert'), may hold values from -0.1875 to 0.1875
Outputs:
- next_acts: bfloat16 [8, 8192, 2048], P('phase', 'expert')
- prev_grads: bfloat16 [8, 8192, 2048], P('phase', 'expert')
- prompt_grads: bfloat16 [8, 2, 10, 2048], P('phase')
The draws below stay inside these ranges and needn't reach their ends.
Inputs may be any that keep to these rules, and one draw needn't show every extreme that they name: `fwd_routes`: each row names 1 different experts; among the 128 tokens of one device no expert is named by more than 18 rows, a bound that some block reaches. `bwd_routes`: each row names 1 different experts; among the 128 tokens of one device no expert is named by more than 18 rows, a bound that some block reaches.
All inputs are finite; a program needn't handle non-finite values.
Results may differ from the reference program's by a relative error of at most 0.008.
Values may be sent and summed in bfloat16 or wider, within the bound.
No kernel may reach another device: no remote copies, remote signals or barrier semaphores. Data moves between devices by JAX's collectives and lax.ppermute only.
A program may use at most 128 MiB of HBM per device.

```python
import math
import jax
import jax.numpy as jnp
import numpy as np
from jax import lax

D = 2048
H = 1024
EXPERTS = 8
TOPK = 1
TENANTS = 2
PLEN = 10
SEGS = 16
TOK_DEV = 128
PHASES = 8
SPLIT = 8
H_DEV = 128
TOKENS = 8192
CAP = 18
N_EXPERT = 64


def touch_ends(result, stream_key, low, largest):
    shape = result.shape
    index_at = [jax.random.randint(jax.random.fold_in(stream_key, axis), (), 0, shape[axis]) for axis in range(len(shape))]
    result = result.at[tuple(index_at)].set(low)
    longest = shape.index(max(shape))
    index_at[longest] = (index_at[longest] + 1) % shape[longest]
    return result.at[tuple(index_at)].set(largest)


def shard_levels(stream_key, dims, shards, least, top_value):
    loudness, own = 1.0, jax.random.fold_in(stream_key, 6)
    for dim, blocks in shards:
        steps = jnp.exp(jax.random.uniform(jax.random.fold_in(own, dim), (blocks,), jnp.float32, least / len(shards), top_value / len(shards)))
        loudness = loudness * jnp.repeat(steps, dims[dim] // blocks).reshape([-1 if axis == dim else 1 for axis in range(len(dims))])
    return loudness


def length_profile(count, total, most, slope):
    portions = [(1 << 20) // math.isqrt(rank ** slope) + 1 for rank in range(2, count + 1)]
    surplus, holding = total - most - (count - 1), [1] * (count - 1)
    while surplus > 0:
        candidates = [i for i in range(count - 1) if holding[i] < most]
        whole, left = sum([portions[i] for i in candidates]), surplus
        for i in candidates:
            extra = min(most - holding[i], max(1, left * portions[i] // whole), surplus)
            holding[i] = holding[i] + extra
            surplus = surplus - extra
    return np.array([most] + holding)


def ragged_sizes(stream_key, count, total, bound, slope):
    if count == 2:
        one = jax.random.randint(stream_key, (), max(1, total - bound), min(bound, total - 1) + 1)
        return jnp.stack([one, total - one])
    tallies = jnp.asarray(length_profile(count, total, bound, slope), jnp.int32)
    couples = (count - 1) // 2
    donor, taker = tallies[1:1 + 2 * couples:2], tallies[2:2 + 2 * couples:2]
    slack = jnp.minimum(donor - 1, bound - taker)
    passed = jax.random.randint(jax.random.fold_in(stream_key, 1), (couples,), 0, 1 << 20) % (slack + 1)
    tallies = tallies.at[1:1 + 2 * couples:2].set(donor - passed).at[2:2 + 2 * couples:2].set(taker + passed)
    return tallies[jax.random.permutation(jax.random.fold_in(stream_key, 2), count)]


def deal_out(rng, own, number, rows, number_of, top, bound, lean):
    order = jax.random.permutation(rng, number_of)
    crowded, usual = shares(number_of, rows * top, bound, lean, True), shares(number_of, rows * top, bound, lean, False)
    places = jnp.arange(number_of)

    def named(sizes, rotation):
        used = int((sizes > 0).sum())
        fixed = max(1, used // 4)
        passed = fixed + (places - fixed + rotation * (used - fixed)) % max(1, number_of - fixed)
        return jnp.zeros((number_of,), jnp.int32).at[order[jnp.where(places < fixed, places, passed)]].set(jnp.asarray(sizes, jnp.int32))

    sizes = jnp.where(number % 4 == 0, named(crowded, number // 4), named(usual, number - number // 4 - 1))
    mixed = jax.random.permutation(jax.random.fold_in(own, 3), number_of)
    giver, sink = mixed[0:number_of // 2 * 2:2], mixed[1:number_of // 2 * 2:2]
    slack = jnp.minimum(sizes[giver] - 1, bound - sizes[sink]) // 2
    slack = jnp.where((giver == order[0]) | (sink == order[0]) | (sizes[sink] == 0), 0, jnp.maximum(slack, 0))
    passed = jax.random.randint(jax.random.fold_in(own, 4), (number_of // 2,), 0, 1 << 20) % (slack + 1)
    sizes = sizes.at[giver].add(-passed).at[sink].add(passed)
    labels = jnp.searchsorted(jnp.cumsum(sizes), jnp.arange(rows * top), side="right").astype(jnp.int32)
    table = labels.reshape(top, rows).T
    table = table[jax.random.permutation(jax.random.fold_in(own, 1), rows)]
    rotation = jax.random.randint(jax.random.fold_in(own, 2), (rows, 1), 0, top)
    return jnp.take_along_axis(table, (jnp.arange(top)[None, :] + rotation) % top, axis=1)


def shares(count, total, reach, slope, full):
    weights = [(1 << 20) // math.isqrt(standing ** slope) + 1 for standing in range(1, count + 1)]
    largest = reach if full else min(reach, max(-(-total // count), total * weights[0] // sum(weights)))
    least = 1 if total - largest >= count - 1 else 0
    given, surplus = [largest] + [least] * (count - 1), total - largest - least * (count - 1)
    while surplus > 0:
        free = [i for i in range(1, count) if given[i] < largest] or [i for i in range(1, count) if given[i] < reach]
        whole, left = sum([weights[i] for i in free]), surplus
        for i in free:
            addition = min(reach - given[i], max(1, left * weights[i] // whole), surplus)
            given[i] = given[i] + addition
            surplus = surplus - addition
    return np.array(given)


def scatter_about(stream_key, dims, scale, bound, split=(), kind=jnp.bfloat16):
    drawn = scale * jax.random.normal(stream_key, dims, jnp.float32)
    if split:
        drawn = drawn * shard_levels(stream_key, dims, split, -0.22, 0.18)
    return jnp.clip(drawn, -bound, bound).astype(kind)


def setup_inputs(seed: int = 0) -> dict:
    splits = jax.random.split(jax.random.key(seed), 17)
    fwd_acts = scatter_about(splits[0], (PHASES, TOKENS, D), 1.0, 6.0, ((0, 8), (1, 64)))
    fwd_routes_keys = jax.random.split(jax.random.fold_in(splits[1], 1), PHASES * TOKENS // TOK_DEV)
    fwd_routes_turns = jax.random.permutation(jax.random.fold_in(splits[1], 3), PHASES * TOKENS // TOK_DEV)
    fwd_routes = jax.vmap(lambda own, number: deal_out(jax.random.fold_in(splits[1], 2), own, number, TOK_DEV, EXPERTS, TOPK, CAP, 2))(fwd_routes_keys, fwd_routes_turns).reshape((PHASES, TOKENS, TOPK))
    fwd_weights = jnp.clip(0.1 + 0.9 * jax.random.uniform(splits[2], (PHASES, TOKENS, TOPK), jnp.float32) ** shard_levels(splits[2], (PHASES, TOKENS, TOPK), ((0, 8), (1, 64)), -0.2, 0.2), 0.1, 1.0)
    fwd_lengths = jax.vmap(lambda own: ragged_sizes(own, SEGS, TOKENS, TOKENS // 4, 2))(jax.random.split(splits[3], PHASES)).reshape((PHASES, SEGS)).astype(jnp.int32)
    fwd_tenants = touch_ends(jax.random.randint(splits[4], (PHASES, SEGS), 0, TENANTS), jax.random.fold_in(splits[4], 1), 0, TENANTS - 1).astype(jnp.int32)
    bwd_acts = scatter_about(splits[5], (PHASES, TOKENS, D), 1.0, 6.0, ((0, 8), (1, 64)))
    bwd_routes_keys = jax.random.split(jax.random.fold_in(splits[6], 1), PHASES * TOKENS // TOK_DEV)
    bwd_routes_turns = jax.random.permutation(jax.random.fold_in(splits[6], 3), PHASES * TOKENS // TOK_DEV)
    bwd_routes = jax.vmap(lambda own, number: deal_out(jax.random.fold_in(splits[6], 2), own, number, TOK_DEV, EXPERTS, TOPK, CAP, 2))(bwd_routes_keys, bwd_routes_turns).reshape((PHASES, TOKENS, TOPK))
    bwd_weights = jnp.clip(0.1 + 0.9 * jax.random.uniform(splits[7], (PHASES, TOKENS, TOPK), jnp.float32) ** shard_levels(splits[7], (PHASES, TOKENS, TOPK), ((0, 8), (1, 64)), -0.2, 0.2), 0.1, 1.0)
    bwd_lengths = jax.vmap(lambda own: ragged_sizes(own, SEGS, TOKENS, TOKENS // 4, 2))(jax.random.split(splits[8], PHASES)).reshape((PHASES, SEGS)).astype(jnp.int32)
    bwd_tenants = touch_ends(jax.random.randint(splits[9], (PHASES, SEGS), 0, TENANTS), jax.random.fold_in(splits[9], 1), 0, TENANTS - 1).astype(jnp.int32)
    bwd_cotangent = scatter_about(splits[10], (PHASES, TOKENS, D), 1.0, 6.0, ((0, 8), (1, 64)))
    prompts = scatter_about(splits[11], (PHASES, TENANTS, PLEN, D), 1.0, 6.0, ((0, 8),))
    norm_gain = jnp.clip(1.0 + 0.18 * jax.random.normal(splits[12], (PHASES, D), jnp.float32), 0.1, 1.9)
    w_gate = scatter_about(splits[13], (PHASES, N_EXPERT, D, H_DEV), D ** -0.5, 0.125, ((0, 8), (1, 64)))
    w_up = scatter_about(splits[14], (PHASES, N_EXPERT, D, H_DEV), D ** -0.5, 0.125, ((0, 8), (1, 64)))
    w_down = scatter_about(splits[15], (PHASES, N_EXPERT, H_DEV, D), H ** -0.5, 0.1875, ((0, 8), (1, 64)))
    return {"fwd_acts": fwd_acts, "fwd_routes": fwd_routes, "fwd_weights": fwd_weights, "fwd_lengths": fwd_lengths, "fwd_tenants": fwd_tenants, "bwd_acts": bwd_acts, "bwd_routes": bwd_routes, "bwd_weights": bwd_weights, "bwd_lengths": bwd_lengths, "bwd_tenants": bwd_tenants, "bwd_cotangent": bwd_cotangent, "prompts": prompts, "norm_gain": norm_gain, "w_gate": w_gate, "w_up": w_up, "w_down": w_down}


EPS = 1e-06

def rounded(values):
    return lax.optimization_barrier(values.astype(jnp.bfloat16)).astype(jnp.float32)

def token_layout(lengths, tenants):
    seg_ends = jnp.cumsum(lengths)
    seg_starts = seg_ends - lengths
    token_index = jnp.arange(TOKENS, dtype=jnp.int32)
    segment = lax.optimization_barrier(jnp.sum((seg_starts[None, :] <= token_index[:, None]).astype(jnp.int32), axis=1)) - 1
    position = token_index - seg_starts[segment]
    return (position, tenants[segment])

def prepare(acts, lengths, tenants, prompts, gain_row):
    position, tenant = token_layout(lengths, tenants)
    prompt_slot = position < PLEN
    prompt_rows = prompts[tenant, jnp.minimum(position, PLEN - 1)]
    inputs = jnp.where(prompt_slot[:, None], prompt_rows, acts)
    widened = inputs.astype(jnp.float32)
    inv_scale = lax.rsqrt(lax.optimization_barrier(jnp.mean(widened * widened, axis=1, keepdims=True)) + EPS)
    normed = (widened * inv_scale * gain_row[None, :]).astype(jnp.bfloat16)
    return (position, tenant, prompt_slot, widened, inv_scale, normed)

def place_rows(routes):
    flattened = routes.reshape(N_EXPERT, TOK_DEV * TOPK)
    onehot = (flattened[:, :, None] == jnp.arange(EXPERTS, dtype=jnp.int32)[None, None, :]).astype(jnp.int32)
    ranking = lax.optimization_barrier(jnp.sum((jnp.cumsum(onehot, axis=1) - 1) * onehot, axis=2))
    blocks = jnp.arange(N_EXPERT, dtype=jnp.int32)[:, None] * CAP
    return (blocks + ranking).reshape(TOKENS, TOPK)

def to_buffers(values, routes, places):
    buffer = jnp.zeros((EXPERTS, N_EXPERT * CAP, values.shape[1]), values.dtype)
    spread = jnp.broadcast_to(values[:, None, :], (TOKENS, TOPK, values.shape[1]))
    return buffer.at[routes, places].set(spread)

def forward_phase(acts, routes, weights, lengths, tenants, prompts, gain_row, gate_all, up_all, down_all):
    position, tenant, prompt_slot, widened, inv_scale, normed = prepare(acts, lengths, tenants, prompts, gain_row)
    places = place_rows(routes)
    buffer = to_buffers(normed, routes, places).astype(jnp.float32)
    summed = jnp.zeros(buffer.shape, jnp.float32)
    for shard in range(SPLIT):
        gate_pre = jnp.einsum('erd,edh->erh', buffer, gate_all[shard].astype(jnp.float32))
        upper = jnp.einsum('erd,edh->erh', buffer, up_all[shard].astype(jnp.float32))
        hidden = rounded(jax.nn.silu(gate_pre) * upper)
        partial_value = jnp.einsum('erh,ehd->erd', hidden, down_all[shard].astype(jnp.float32))
        summed = summed + rounded(partial_value)
    gathered = summed[routes, places]
    mixed_out = widened + lax.optimization_barrier(jnp.sum(weights[:, :, None] * gathered, axis=1))
    return mixed_out.astype(jnp.bfloat16)

def backward_phase(acts, routes, weights, lengths, tenants, cotangent, prompts, gain_row, gate_all, up_all, down_all):
    position, tenant, prompt_slot, widened, inv_scale, normed = prepare(acts, lengths, tenants, prompts, gain_row)
    places = place_rows(routes)
    buffer = to_buffers(normed, routes, places).astype(jnp.float32)
    cot_buffer = to_buffers(cotangent, routes, places).astype(jnp.float32)
    summed = jnp.zeros(buffer.shape, jnp.float32)
    for shard in range(SPLIT):
        gate_w = gate_all[shard].astype(jnp.float32)
        up_w = up_all[shard].astype(jnp.float32)
        gate_pre = jnp.einsum('erd,edh->erh', buffer, gate_w)
        upper = jnp.einsum('erd,edh->erh', buffer, up_w)
        hidden_grad = jnp.einsum('erd,ehd->erh', cot_buffer, down_all[shard].astype(jnp.float32))
        sigmoid_gate = jax.nn.sigmoid(gate_pre)
        gate_grad = rounded(hidden_grad * upper * sigmoid_gate * (1.0 + gate_pre * (1.0 - sigmoid_gate)))
        up_grad = rounded(hidden_grad * (gate_pre * sigmoid_gate))
        partial_value = jnp.einsum('erh,edh->erd', gate_grad, gate_w) + jnp.einsum('erh,edh->erd', up_grad, up_w)
        summed = summed + rounded(partial_value)
    gathered = summed[routes, places]
    normed_grad = lax.optimization_barrier(jnp.sum(weights[:, :, None] * gathered, axis=1))
    scaled = normed_grad * gain_row[None, :]
    inner = lax.optimization_barrier(jnp.mean(widened * scaled, axis=1, keepdims=True))
    input_grad = cotangent.astype(jnp.float32) + inv_scale * scaled - widened * inv_scale ** 3 * inner
    to_prev = jnp.where(prompt_slot[:, None], 0.0, input_grad).astype(jnp.bfloat16)
    kept = jnp.where(prompt_slot[:, None], input_grad, 0.0)
    prompt_sum = jnp.zeros((TENANTS, PLEN, input_grad.shape[1]), jnp.float32)
    prompt_sum = prompt_sum.at[tenant, jnp.minimum(position, PLEN - 1)].add(kept)
    return (to_prev, prompt_sum.astype(jnp.bfloat16))

def reference(fwd_acts, fwd_routes, fwd_weights, fwd_lengths, fwd_tenants, bwd_acts, bwd_routes, bwd_weights, bwd_lengths, bwd_tenants, bwd_cotangent, prompts, norm_gain, w_gate, w_up, w_down):
    leaving_all = []
    prev_all = []
    prompt_all = []
    for phase_idx in range(PHASES):
        gate_all = w_gate[phase_idx].reshape(SPLIT, EXPERTS, D, H_DEV)
        up_all = w_up[phase_idx].reshape(SPLIT, EXPERTS, D, H_DEV)
        down_all = w_down[phase_idx].reshape(SPLIT, EXPERTS, H_DEV, D)
        leaving_all.append(forward_phase(fwd_acts[phase_idx], fwd_routes[phase_idx], fwd_weights[phase_idx], fwd_lengths[phase_idx], fwd_tenants[phase_idx], prompts[phase_idx], norm_gain[phase_idx], gate_all, up_all, down_all))
        to_prev, prompt_grad = backward_phase(bwd_acts[phase_idx], bwd_routes[phase_idx], bwd_weights[phase_idx], bwd_lengths[phase_idx], bwd_tenants[phase_idx], bwd_cotangent[phase_idx], prompts[phase_idx], norm_gain[phase_idx], gate_all, up_all, down_all)
        prev_all.append(to_prev)
        prompt_all.append(prompt_grad)
    blank = jnp.zeros((1, TOKENS, D), jnp.bfloat16)
    leaving = jnp.stack(leaving_all)
    previous = jnp.stack(prev_all)
    next_acts = jnp.concatenate([blank, leaving[:-1]], axis=0)
    prev_grads = jnp.concatenate([previous[1:], blank], axis=0)
    return (next_acts, prev_grads, jnp.stack(prompt_all))
```

```python
import functools

import jax
import jax.numpy as jnp
from jax import lax
from jax.experimental import pallas as pl
from jax.experimental.pallas import tpu as pltpu
from jax.sharding import Mesh, PartitionSpec as P

EXPERTS = 8
TENANTS = 2
PLEN = 10
SLOTS = TENANTS * PLEN
CAP = 18
ROWS = 40
COT_ROWS = 24
BLOCK = ROWS + COT_ROWS
FWD_AT = 16
EXTRA = 128
NO_SLOT = 31

EPS = 1e-06
BF16 = jnp.bfloat16
F32 = jnp.float32


def token_layout(lengths, tenants, first_row, tok_count):
    count = lengths.shape[0]
    token_index = first_row + jnp.arange(tok_count, dtype=jnp.int32)
    order = jnp.arange(count, dtype=jnp.int32)
    earlier = order[:, None] < order[None, :]
    seg_starts = jnp.sum(jnp.where(earlier, lengths[:, None], 0), axis=0)
    seg_ends = seg_starts + lengths
    chosen = (seg_starts[None, :] <= token_index[:, None]) & (token_index[:, None] < seg_ends[None, :])
    position = token_index - jnp.sum(jnp.where(chosen, seg_starts[None, :], 0), axis=1)
    tenant = jnp.sum(jnp.where(chosen, tenants[None, :], 0), axis=1)
    return position, tenant


def prepare(acts, lengths, tenants, flat_table, gain_row, first_row):
    tok_count = acts.shape[0]
    position, tenant = token_layout(lengths, tenants, first_row, tok_count)
    prompt_slot = position < PLEN
    slot = jnp.where(prompt_slot, tenant * PLEN + position, NO_SLOT)
    selector = slot[:, None] == jnp.arange(SLOTS, dtype=jnp.int32)[None, :]
    prompt_rows = jnp.dot(selector.astype(BF16), flat_table, preferred_element_type=F32).astype(BF16)
    inputs = jnp.where(prompt_slot[:, None], prompt_rows, acts)
    widened = inputs.astype(F32)
    inv_scale = lax.rsqrt(jnp.mean(widened * widened, axis=1, keepdims=True) + EPS)
    normed = (widened * inv_scale * gain_row[None, :]).astype(BF16)
    return inputs, inv_scale, normed, prompt_slot, slot, selector


def ranks(routes):
    tok_count = routes.shape[0]
    at = jnp.arange(tok_count, dtype=jnp.int32)
    same = (routes[None, :] == routes[:, None]) & (at[None, :] < at[:, None])
    return jnp.sum(same.astype(jnp.int32), axis=1)


def expert_kernel(parts, has_acc, final, *refs):
    x_ref, c_ref = refs[:2]
    at = 2
    shards = []
    for count in parts:
        shards.append((refs[at : at + count], refs[at + count : at + 2 * count]))
        at += 2 * count
    acc_ref = None
    if has_acc:
        acc_ref = refs[at]
        at += 1
    out_ref = refs[at]
    total = refs[at + 1] if final else out_ref
    blocks = x_ref.shape[0] // ROWS
    width = x_ref.shape[1]
    step = 512
    contract = (((1,), (1,)), ((), ()))
    row = lax.broadcasted_iota(jnp.int32, (blocks, ROWS - FWD_AT, 1), 1) + FWD_AT
    is_fwd = (row >= CAP) & (row < 2 * CAP)

    for number, (gu_refs, d_refs) in enumerate(shards):
        depth = width // len(gu_refs)
        gu_out = None
        for k, ref in enumerate(gu_refs):
            piece = jnp.dot(
                x_ref[:, k * depth : (k + 1) * depth], ref[...], preferred_element_type=F32
            )
            gu_out = piece if gu_out is None else gu_out + piece
        if len(d_refs) == 1:
            down = d_refs[0][...]
        else:
            down = jnp.concatenate([ref[...] for ref in d_refs], axis=0)
        half = gu_out.shape[1] // 2
        hidden_grad = lax.dot_general(c_ref[...], down, contract, preferred_element_type=F32)
        gate = gu_out[:, :half].reshape(blocks, ROWS, half)
        upper = gu_out[:, half:].reshape(blocks, ROWS, half)
        gate_f, up_f = gate[:, FWD_AT:], upper[:, FWD_AT:]
        hidden = gate_f / (1.0 + jnp.exp(-gate_f)) * up_f
        hidden = jnp.where(is_fwd, hidden, 0.0)
        hidden = hidden.reshape(blocks * (ROWS - FWD_AT), half).astype(BF16)
        gate_b = gate[:, :COT_ROWS].reshape(blocks * COT_ROWS, half)
        up_b = upper[:, :COT_ROWS].reshape(blocks * COT_ROWS, half)
        sig = 1.0 / (1.0 + jnp.exp(-gate_b))
        gate_grad = hidden_grad * up_b * sig * (1.0 + gate_b * (1.0 - sig))
        up_grad = hidden_grad * (gate_b * sig)
        grads = jnp.concatenate([gate_grad.astype(BF16), up_grad.astype(BF16)], axis=1)
        first = number == 0 and not has_acc
        last = final and number == len(shards) - 1
        for n in range(width // step):
            cols = slice(n * step, (n + 1) * step)
            part, inner = divmod(n * step, depth)
            gu_rows = gu_refs[part][inner : inner + step, :]
            back = lax.dot_general(grads, gu_rows, contract, preferred_element_type=F32)
            fwd = jnp.dot(hidden, down[:, cols], preferred_element_type=F32)
            back = back.reshape(blocks, COT_ROWS, step)
            fwd = fwd.reshape(blocks, ROWS - FWD_AT, step)
            pieces = [
                back[:, :FWD_AT],
                back[:, FWD_AT:] + fwd[:, : COT_ROWS - FWD_AT],
                fwd[:, COT_ROWS - FWD_AT :],
            ]
            value = jnp.concatenate(pieces, axis=1).reshape(blocks * ROWS, step)
            if not first:
                source = acc_ref if number == 0 else total
                value = value + source[:, cols]
            if last:
                out_ref[:, cols] = value.astype(out_ref.dtype)
            else:
                total[:, cols] = value


def expert_step(rows, cots, shards, acc, final):
    parts = tuple(len(gu) for gu, _ in shards)
    operands = [rows, cots]
    for gu, d in shards:
        operands += list(gu) + list(d)
    if acc is not None:
        operands.append(acc)
    shape = rows.shape
    whole = pl.BlockSpec(memory_space=pltpu.VMEM)
    scratch = [pltpu.VMEM(shape, F32)] if final else []
    return pl.pallas_call(
        functools.partial(expert_kernel, parts, acc is not None, final),
        out_shape=jax.ShapeDtypeStruct(shape, BF16 if final else F32),
        in_specs=[whole] * len(operands),
        out_specs=whole,
        scratch_shapes=scratch,
        compiler_params=pltpu.CompilerParams(vmem_limit_bytes=40 * 1024 * 1024),
    )(*operands)


def rotated(value, axis, distance):
    size = lax.axis_size(axis)
    return lax.ppermute(value, axis, [(i, (i + distance) % size) for i in range(size)])


def shifted(block, axis, distance):
    size = lax.axis_size(axis)
    route = [(i, i + distance) for i in range(size) if 0 <= i + distance < size]
    return lax.ppermute(block, axis, route)


def summed(value, axis):
    size = lax.axis_size(axis)
    distance = 1
    while distance < size:
        other = lax.ppermute(value.astype(BF16), axis, [(i, i ^ distance) for i in range(size)])
        value = value.astype(BF16).astype(F32) + other.astype(F32)
        distance *= 2
    return value


def on_device(
    fwd_acts,
    fwd_routes,
    fwd_weights,
    fwd_lengths,
    fwd_tenants,
    bwd_acts,
    bwd_routes,
    bwd_weights,
    bwd_lengths,
    bwd_tenants,
    bwd_cotangent,
    prompts,
    norm_gain,
    w_gate,
    w_up,
    w_down,
):
    tok_count, width = fwd_acts.shape[1:]
    gain_row = norm_gain[0]
    flat_table = prompts[0].reshape(SLOTS, width)
    splits = lax.axis_size("split")

    own_gu = jnp.concatenate([w_gate[0, 0], w_up[0, 0]], axis=1)
    own_d = w_down[0, 0]
    rounds = []
    gu_a = gu_b = own_gu
    d_a = d_b = own_d
    for _ in range(splits // 2 - 1):
        gu_a, gu_b = rotated(gu_a, "split", 1), rotated(gu_b, "split", -1)
        d_a, d_b = rotated(d_a, "split", 1), rotated(d_b, "split", -1)
        rounds.append([((gu_a,), (d_a,)), ((gu_b,), (d_b,))])
    half_k, half_h = width // 2, own_d.shape[0] // 2
    last = (
        (rotated(gu_a[:half_k], "split", 1), rotated(gu_b[half_k:], "split", -1)),
        (rotated(d_a[:half_h], "split", 1), rotated(d_b[half_h:], "split", -1)),
    )

    first_row = (lax.axis_index("split") * lax.axis_size("column") + lax.axis_index("column")) * tok_count
    fwd_in, _, fwd_normed, _, _, _ = prepare(
        fwd_acts[0], fwd_lengths[0], fwd_tenants[0], flat_table, gain_row, first_row
    )
    bwd_in, bwd_scale, bwd_normed, bwd_slot, slot, selector = prepare(
        bwd_acts[0], bwd_lengths[0], bwd_tenants[0], flat_table, gain_row, first_row
    )
    cotangent = bwd_cotangent[0]
    f_route, b_route = fwd_routes[0, :, 0], bwd_routes[0, :, 0]
    f_rank, b_rank = ranks(f_route), ranks(b_route)
    weight_b = bwd_weights[0, :, 0]
    high = lax.reduce_precision(weight_b, 8, 7)
    low = weight_b - high
    lane = jnp.arange(EXTRA, dtype=jnp.int32)[None, :]
    extra = jnp.where(lane == 0, high[:, None], 0.0)
    extra = jnp.where(lane == 1, low[:, None], extra)
    extra = jnp.where(lane == 2, slot.astype(F32)[:, None], extra).astype(BF16)
    blank = jnp.zeros((tok_count, EXTRA), BF16)
    sources = jnp.concatenate(
        [
            jnp.concatenate([bwd_normed, extra], axis=1),
            jnp.concatenate([fwd_normed, blank], axis=1),
            jnp.concatenate([cotangent, blank], axis=1),
        ],
        axis=0,
    )
    target = jnp.concatenate(
        [
            b_route * BLOCK + b_rank,
            f_route * BLOCK + CAP + f_rank,
            b_route * BLOCK + ROWS + b_rank,
        ]
    )
    picker = target[None, :] == jnp.arange(EXPERTS * BLOCK, dtype=jnp.int32)[:, None]
    packed = jnp.dot(picker.astype(BF16), sources, preferred_element_type=F32).astype(BF16)
    packed = packed.reshape(EXPERTS, BLOCK, width + EXTRA)
    arrived = lax.all_to_all(packed, "column", split_axis=0, concat_axis=0, tiled=True)
    rows = arrived[:, :ROWS, :width].reshape(EXPERTS * ROWS, width)
    cots = arrived[:, ROWS:, :width].reshape(EXPERTS * COT_ROWS, width)
    notes = arrived[:, :ROWS, width : width + 3].astype(F32).reshape(EXPERTS * ROWS, 3)

    acc = expert_step(rows, cots, [((own_gu,), (own_d,))] + rounds[0] + rounds[1], None, False)
    for pair in rounds[2:]:
        acc = expert_step(rows, cots, pair, acc, False)
    partial = expert_step(rows, cots, [last], acc, True)

    returned = lax.all_to_all(
        partial.reshape(EXPERTS, ROWS, width), "column", split_axis=0, concat_axis=0, tiled=True
    ).reshape(EXPERTS * ROWS, width)

    slot_iota = jnp.arange(SLOTS, dtype=F32)[:, None]
    at_slot = notes[:, 2][None, :] == slot_iota
    weighing = jnp.concatenate(
        [jnp.where(at_slot, notes[:, 0][None, :], 0.0), jnp.where(at_slot, notes[:, 1][None, :], 0.0)], axis=0
    ).astype(BF16)
    both = jnp.dot(weighing, partial, preferred_element_type=F32)
    slot_q = (both[:SLOTS] + both[SLOTS:]) * gain_row[None, :]
    slot_in = flat_table.astype(F32)
    slot_scale = lax.rsqrt(jnp.mean(slot_in * slot_in, axis=1, keepdims=True) + EPS)
    slot_inner = jnp.mean(slot_in * slot_q, axis=1, keepdims=True)
    slot_cot = jnp.dot(jnp.transpose(selector.astype(BF16)), cotangent, preferred_element_type=F32)
    local_sums = slot_cot + slot_scale * slot_q - slot_in * slot_scale**3 * slot_inner
    totals = summed(summed(local_sums, "column"), "split")
    prompt_grads = totals.astype(BF16).reshape(1, TENANTS, PLEN, width)

    home = jnp.arange(EXPERTS * ROWS, dtype=jnp.int32)[None, :]
    f_take = ((f_route * ROWS + CAP + f_rank)[:, None] == home).astype(BF16)
    b_take = ((b_route * ROWS + b_rank)[:, None] == home).astype(BF16)
    f_out = jnp.dot(f_take, returned, preferred_element_type=F32)
    leaving = (fwd_in.astype(F32) + fwd_weights[0] * f_out).astype(BF16)
    next_acts = shifted(leaving, "phase", 1)
    back_out = jnp.dot(b_take, returned, preferred_element_type=F32)
    scaled = bwd_weights[0] * back_out * gain_row[None, :]
    wide = bwd_in.astype(F32)
    inner = jnp.mean(wide * scaled, axis=1, keepdims=True)
    input_grad = cotangent.astype(F32) + bwd_scale * scaled - wide * bwd_scale**3 * inner
    to_prev = jnp.where(bwd_slot[:, None], 0.0, input_grad).astype(BF16)
    prev_grads = shifted(to_prev, "phase", -1)
    return next_acts[None], prev_grads[None], prompt_grads


def solution(mesh):
    names = mesh.axis_names
    phases, experts = mesh.shape[names[0]], mesh.shape[names[1]]
    grid = mesh.devices.reshape(phases, experts // EXPERTS, EXPERTS)
    inner = Mesh(grid, ("phase", "split", "column"))
    both = ("split", "column")
    tokens = P("phase", both, None)
    per_phase = P("phase", None)
    weights = P("phase", both, None, None)
    table = P("phase", None, None, None)
    placed = (
        tokens,
        tokens,
        tokens,
        per_phase,
        per_phase,
        tokens,
        tokens,
        tokens,
        per_phase,
        per_phase,
        tokens,
        table,
        per_phase,
        weights,
        weights,
        weights,
    )
    return jax.shard_map(
        on_device,
        mesh=inner,
        in_specs=placed,
        out_specs=(tokens, tokens, table),
        check_vma=False,
    )
```

```python
import functools

import jax
import jax.numpy as jnp
from jax import lax
from jax.experimental import pallas as pl
from jax.experimental.pallas import tpu as pltpu
from jax.sharding import Mesh, PartitionSpec as P

EXPERTS = 8
TENANTS = 2
PLEN = 10
SLOTS = TENANTS * PLEN
CAP = 18
ROWS = 40
COT_ROWS = 24
BLOCK = ROWS + COT_ROWS
FWD_AT = 16
EXTRA = 128
NO_SLOT = 31

EPS = 1e-06
BF16 = jnp.bfloat16
F32 = jnp.float32


def token_layout(lengths, tenants, first_row, tok_count):
    count = lengths.shape[0]
    token_index = first_row + jnp.arange(tok_count, dtype=jnp.int32)
    order = jnp.arange(count, dtype=jnp.int32)
    earlier = order[:, None] < order[None, :]
    seg_starts = jnp.sum(jnp.where(earlier, lengths[:, None], 0), axis=0)
    seg_ends = seg_starts + lengths
    chosen = (seg_starts[None, :] <= token_index[:, None]) & (token_index[:, None] < seg_ends[None, :])
    position = token_index - jnp.sum(jnp.where(chosen, seg_starts[None, :], 0), axis=1)
    tenant = jnp.sum(jnp.where(chosen, tenants[None, :], 0), axis=1)
    return position, tenant


def prepare(acts, lengths, tenants, flat_table, gain_row, first_row):
    tok_count = acts.shape[0]
    position, tenant = token_layout(lengths, tenants, first_row, tok_count)
    prompt_slot = position < PLEN
    slot = jnp.where(prompt_slot, tenant * PLEN + position, NO_SLOT)
    selector = slot[:, None] == jnp.arange(SLOTS, dtype=jnp.int32)[None, :]
    prompt_rows = jnp.dot(selector.astype(BF16), flat_table, preferred_element_type=F32).astype(BF16)
    inputs = jnp.where(prompt_slot[:, None], prompt_rows, acts)
    widened = inputs.astype(F32)
    inv_scale = lax.rsqrt(jnp.mean(widened * widened, axis=1, keepdims=True) + EPS)
    normed = (widened * inv_scale * gain_row[None, :]).astype(BF16)
    return inputs, inv_scale, normed, prompt_slot, slot, selector


def ranks(routes):
    tok_count = routes.shape[0]
    at = jnp.arange(tok_count, dtype=jnp.int32)
    same = (routes[None, :] == routes[:, None]) & (at[None, :] < at[:, None])
    return jnp.sum(same.astype(jnp.int32), axis=1)


def expert_kernel(parts, has_acc, final, *refs):
    x_ref, c_ref = refs[:2]
    at = 2
    shards = []
    for count in parts:
        shards.append((refs[at : at + count], refs[at + count : at + 2 * count]))
        at += 2 * count
    acc_ref = None
    if has_acc:
        acc_ref = refs[at]
        at += 1
    out_ref = refs[at]
    total = refs[at + 1] if final else out_ref
    blocks = x_ref.shape[0] // ROWS
    width = x_ref.shape[1]
    step = 512
    contract = (((1,), (1,)), ((), ()))
    row = lax.broadcasted_iota(jnp.int32, (blocks, ROWS - FWD_AT, 1), 1) + FWD_AT
    is_fwd = (row >= CAP) & (row < 2 * CAP)

    for number, (gu_refs, d_refs) in enumerate(shards):
        depth = width // len(gu_refs)
        gu_out = None
        for k, ref in enumerate(gu_refs):
            piece = jnp.dot(
                x_ref[:, k * depth : (k + 1) * depth], ref[...], preferred_element_type=F32
            )
            gu_out = piece if gu_out is None else gu_out + piece
        if len(d_refs) == 1:
            down = d_refs[0][...]
        else:
            down = jnp.concatenate([ref[...] for ref in d_refs], axis=0)
        half = gu_out.shape[1] // 2
        hidden_grad = lax.dot_general(c_ref[...], down, contract, preferred_element_type=F32)
        gate = gu_out[:, :half].reshape(blocks, ROWS, half)
        upper = gu_out[:, half:].reshape(blocks, ROWS, half)
        gate_f, up_f = gate[:, FWD_AT:], upper[:, FWD_AT:]
        hidden = gate_f / (1.0 + jnp.exp(-gate_f)) * up_f
        hidden = jnp.where(is_fwd, hidden, 0.0)
        hidden = hidden.reshape(blocks * (ROWS - FWD_AT), half).astype(BF16)
        gate_b = gate[:, :COT_ROWS].reshape(blocks * COT_ROWS, half)
        up_b = upper[:, :COT_ROWS].reshape(blocks * COT_ROWS, half)
        sig = 1.0 / (1.0 + jnp.exp(-gate_b))
        gate_grad = hidden_grad * up_b * sig * (1.0 + gate_b * (1.0 - sig))
        up_grad = hidden_grad * (gate_b * sig)
        grads = jnp.concatenate([gate_grad.astype(BF16), up_grad.astype(BF16)], axis=1)
        first = number == 0 and not has_acc
        last = final and number == len(shards) - 1
        for n in range(width // step):
            cols = slice(n * step, (n + 1) * step)
            part, inner = divmod(n * step, depth)
            gu_rows = gu_refs[part][inner : inner + step, :]
            back = lax.dot_general(grads, gu_rows, contract, preferred_element_type=F32)
            fwd = jnp.dot(hidden, down[:, cols], preferred_element_type=F32)
            back = back.reshape(blocks, COT_ROWS, step)
            fwd = fwd.reshape(blocks, ROWS - FWD_AT, step)
            pieces = [
                back[:, :FWD_AT],
                back[:, FWD_AT:] + fwd[:, : COT_ROWS - FWD_AT],
                fwd[:, COT_ROWS - FWD_AT :],
            ]
            value = jnp.concatenate(pieces, axis=1).reshape(blocks * ROWS, step)
            if not first:
                source = acc_ref if number == 0 else total
                value = value + source[:, cols]
            if last:
                out_ref[:, cols] = value.astype(out_ref.dtype)
            else:
                total[:, cols] = value


def w_hidden(shards):
    return sum(d.shape[0] for _, ds in shards for d in ds)


def expert_step(rows, cots, shards, acc, final):
    parts = tuple(len(gu) for gu, _ in shards)
    operands = [rows, cots]
    for gu, d in shards:
        operands += list(gu) + list(d)
    if acc is not None:
        operands.append(acc)
    shape = rows.shape
    whole = pl.BlockSpec(memory_space=pltpu.VMEM)
    scratch = [pltpu.VMEM(shape, F32)] if final else []
    hidden = w_hidden(shards)
    cost = pl.CostEstimate(
        flops=2 * hidden * shape[1] * (2 * shape[0] + 4 * cots.shape[0]),
        transcendentals=hidden * 2 * cots.shape[0],
        bytes_accessed=sum(o.size * o.dtype.itemsize for o in operands) + 4 * rows.size,
    )
    return pl.pallas_call(
        functools.partial(expert_kernel, parts, acc is not None, final),
        out_shape=jax.ShapeDtypeStruct(shape, BF16 if final else F32),
        in_specs=[whole] * len(operands),
        out_specs=whole,
        scratch_shapes=scratch,
        compiler_params=pltpu.CompilerParams(vmem_limit_bytes=40 * 1024 * 1024),
        cost_estimate=cost,
    )(*operands)


def rotated(value, axis, distance):
    size = lax.axis_size(axis)
    return lax.ppermute(value, axis, [(i, (i + distance) % size) for i in range(size)])


def shifted(block, axis, distance):
    size = lax.axis_size(axis)
    route = [(i, i + distance) for i in range(size) if 0 <= i + distance < size]
    return lax.ppermute(block, axis, route)


def summed(value, axis):
    size = lax.axis_size(axis)
    distance = 1
    while distance < size:
        other = lax.ppermute(value.astype(BF16), axis, [(i, i ^ distance) for i in range(size)])
        value = value.astype(BF16).astype(F32) + other.astype(F32)
        distance *= 2
    return value


def on_device(
    fwd_acts,
    fwd_routes,
    fwd_weights,
    fwd_lengths,
    fwd_tenants,
    bwd_acts,
    bwd_routes,
    bwd_weights,
    bwd_lengths,
    bwd_tenants,
    bwd_cotangent,
    prompts,
    norm_gain,
    w_gate,
    w_up,
    w_down,
):
    tok_count, width = fwd_acts.shape[1:]
    gain_row = norm_gain[0]
    flat_table = prompts[0].reshape(SLOTS, width)
    splits = lax.axis_size("split")

    own_gu = jnp.concatenate([w_gate[0, 0], w_up[0, 0]], axis=1)
    own_d = w_down[0, 0]
    rounds = []
    gu_a = gu_b = own_gu
    d_a = d_b = own_d
    for _ in range(splits // 2 - 1):
        d_a, d_b = rotated(d_a, "split", 1), rotated(d_b, "split", -1)
        gu_a, gu_b = rotated(gu_a, "split", 1), rotated(gu_b, "split", -1)
        rounds.append([((gu_a,), (d_a,)), ((gu_b,), (d_b,))])

    first_row = (lax.axis_index("split") * lax.axis_size("column") + lax.axis_index("column")) * tok_count
    fwd_in, _, fwd_normed, _, _, _ = prepare(
        fwd_acts[0], fwd_lengths[0], fwd_tenants[0], flat_table, gain_row, first_row
    )
    bwd_in, bwd_scale, bwd_normed, bwd_slot, slot, selector = prepare(
        bwd_acts[0], bwd_lengths[0], bwd_tenants[0], flat_table, gain_row, first_row
    )
    cotangent = bwd_cotangent[0]
    f_route, b_route = fwd_routes[0, :, 0], bwd_routes[0, :, 0]
    f_rank, b_rank = ranks(f_route), ranks(b_route)
    weight_b = bwd_weights[0, :, 0]
    high = lax.reduce_precision(weight_b, 8, 7)
    low = weight_b - high
    lane = jnp.arange(EXTRA, dtype=jnp.int32)[None, :]
    extra = jnp.where(lane == 0, high[:, None], 0.0)
    extra = jnp.where(lane == 1, low[:, None], extra)
    extra = jnp.where(lane == 2, slot.astype(F32)[:, None], extra).astype(BF16)
    blank = jnp.zeros((tok_count, EXTRA), BF16)
    sources = jnp.concatenate(
        [
            jnp.concatenate([bwd_normed, extra], axis=1),
            jnp.concatenate([fwd_normed, blank], axis=1),
            jnp.concatenate([cotangent, blank], axis=1),
        ],
        axis=0,
    )
    target = jnp.concatenate(
        [
            b_route * BLOCK + b_rank,
            f_route * BLOCK + CAP + f_rank,
            b_route * BLOCK + ROWS + b_rank,
        ]
    )
    picker = target[None, :] == jnp.arange(EXPERTS * BLOCK, dtype=jnp.int32)[:, None]
    packed = jnp.dot(picker.astype(BF16), sources, preferred_element_type=F32).astype(BF16)
    packed = packed.reshape(EXPERTS, BLOCK, width + EXTRA)
    packed, _ = lax.optimization_barrier((packed, rounds[0][0][1][0]))
    arrived = lax.all_to_all(packed, "column", split_axis=0, concat_axis=0, tiled=True)
    rows = arrived[:, :ROWS, :width].reshape(EXPERTS * ROWS, width)
    cots = arrived[:, ROWS:, :width].reshape(EXPERTS * COT_ROWS, width)
    notes = arrived[:, :ROWS, width : width + 3].astype(F32).reshape(EXPERTS * ROWS, 3)

    acc = expert_step(rows, cots, [((own_gu,), (own_d,))] + rounds[0] + rounds[1], None, False)
    half_k, half_h = width // 2, own_d.shape[0] // 2
    halves = (gu_a[:half_k], gu_b[half_k:], d_a[:half_h], d_b[half_h:])
    last = (
        (rotated(halves[0], "split", 1), rotated(halves[1], "split", -1)),
        (rotated(halves[2], "split", 1), rotated(halves[3], "split", -1)),
    )
    for pair in rounds[2:]:
        acc = expert_step(rows, cots, pair, acc, False)
    partial = expert_step(rows, cots, [last], acc, True)

    returned = lax.all_to_all(
        partial.reshape(EXPERTS, ROWS, width), "column", split_axis=0, concat_axis=0, tiled=True
    ).reshape(EXPERTS * ROWS, width)

    slot_iota = jnp.arange(SLOTS, dtype=F32)[:, None]
    at_slot = notes[:, 2][None, :] == slot_iota
    weighing = jnp.concatenate(
        [jnp.where(at_slot, notes[:, 0][None, :], 0.0), jnp.where(at_slot, notes[:, 1][None, :], 0.0)], axis=0
    ).astype(BF16)
    both = jnp.dot(weighing, partial, preferred_element_type=F32)
    slot_q = (both[:SLOTS] + both[SLOTS:]) * gain_row[None, :]
    slot_in = flat_table.astype(F32)
    slot_scale = lax.rsqrt(jnp.mean(slot_in * slot_in, axis=1, keepdims=True) + EPS)
    slot_inner = jnp.mean(slot_in * slot_q, axis=1, keepdims=True)
    slot_cot = jnp.dot(jnp.transpose(selector.astype(BF16)), cotangent, preferred_element_type=F32)
    local_sums = slot_cot + slot_scale * slot_q - slot_in * slot_scale**3 * slot_inner
    totals = summed(summed(local_sums, "split"), "column")
    prompt_grads = totals.astype(BF16).reshape(1, TENANTS, PLEN, width)

    home = jnp.arange(EXPERTS * ROWS, dtype=jnp.int32)[None, :]
    f_take = ((f_route * ROWS + CAP + f_rank)[:, None] == home).astype(BF16)
    b_take = ((b_route * ROWS + b_rank)[:, None] == home).astype(BF16)
    f_out = jnp.dot(f_take, returned, preferred_element_type=F32)
    leaving = (fwd_in.astype(F32) + fwd_weights[0] * f_out).astype(BF16)
    next_acts = shifted(leaving, "phase", 1)
    back_out = jnp.dot(b_take, returned, preferred_element_type=F32)
    scaled = bwd_weights[0] * back_out * gain_row[None, :]
    wide = bwd_in.astype(F32)
    inner = jnp.mean(wide * scaled, axis=1, keepdims=True)
    input_grad = cotangent.astype(F32) + bwd_scale * scaled - wide * bwd_scale**3 * inner
    to_prev = jnp.where(bwd_slot[:, None], 0.0, input_grad).astype(BF16)
    prev_grads = shifted(to_prev, "phase", -1)
    return next_acts[None], prev_grads[None], prompt_grads


def solution(mesh):
    names = mesh.axis_names
    phases, experts = mesh.shape[names[0]], mesh.shape[names[1]]
    grid = mesh.devices.reshape(phases, experts // EXPERTS, EXPERTS)
    inner = Mesh(grid, ("phase", "split", "column"))
    both = ("split", "column")
    tokens = P("phase", both, None)
    per_phase = P("phase", None)
    weights = P("phase", both, None, None)
    table = P("phase", None, None, None)
    placed = (
        tokens,
        tokens,
        tokens,
        per_phase,
        per_phase,
        tokens,
        tokens,
        tokens,
        per_phase,
        per_phase,
        tokens,
        table,
        per_phase,
        weights,
        weights,
        weights,
    )
    return jax.shard_map(
        on_device,
        mesh=inner,
        in_specs=placed,
        out_specs=(tokens, tokens, table),
        check_vma=False,
    )
```

```python
import functools

import jax
import jax.numpy as jnp
from jax import lax
from jax.experimental import pallas as pl
from jax.experimental.pallas import tpu as pltpu
from jax.sharding import Mesh, PartitionSpec as P

EXPERTS = 8
TENANTS = 2
PLEN = 10
SLOTS = TENANTS * PLEN
CAP = 18
ROWS = 40
COT_ROWS = 24
BLOCK = ROWS + COT_ROWS
FWD_AT = 16
EXTRA = 128
NO_SLOT = 31

EPS = 1e-06
BF16 = jnp.bfloat16
F32 = jnp.float32


def token_layout(lengths, tenants, first_row, tok_count):
    count = lengths.shape[0]
    token_index = first_row + jnp.arange(tok_count, dtype=jnp.int32)
    order = jnp.arange(count, dtype=jnp.int32)
    earlier = order[:, None] < order[None, :]
    seg_starts = jnp.sum(jnp.where(earlier, lengths[:, None], 0), axis=0)
    seg_ends = seg_starts + lengths
    chosen = (seg_starts[None, :] <= token_index[:, None]) & (token_index[:, None] < seg_ends[None, :])
    position = token_index - jnp.sum(jnp.where(chosen, seg_starts[None, :], 0), axis=1)
    tenant = jnp.sum(jnp.where(chosen, tenants[None, :], 0), axis=1)
    return position, tenant


def prepare(acts, lengths, tenants, flat_table, gain_row, first_row):
    tok_count = acts.shape[0]
    position, tenant = token_layout(lengths, tenants, first_row, tok_count)
    prompt_slot = position < PLEN
    slot = jnp.where(prompt_slot, tenant * PLEN + position, NO_SLOT)
    selector = slot[:, None] == jnp.arange(SLOTS, dtype=jnp.int32)[None, :]
    prompt_rows = jnp.dot(selector.astype(BF16), flat_table, preferred_element_type=F32).astype(BF16)
    inputs = jnp.where(prompt_slot[:, None], prompt_rows, acts)
    widened = inputs.astype(F32)
    inv_scale = lax.rsqrt(jnp.mean(widened * widened, axis=1, keepdims=True) + EPS)
    normed = (widened * inv_scale * gain_row[None, :]).astype(BF16)
    return inputs, inv_scale, normed, prompt_slot, slot, selector


def ranks(routes):
    tok_count = routes.shape[0]
    at = jnp.arange(tok_count, dtype=jnp.int32)
    same = (routes[None, :] == routes[:, None]) & (at[None, :] < at[:, None])
    return jnp.sum(same.astype(jnp.int32), axis=1)


def expert_kernel(parts, has_acc, final, *refs):
    refs = list(refs)
    x_ref, c_ref = refs.pop(0), refs.pop(0)
    sources = []
    for count in parts:
        sources.append((refs[:count], refs[count : 2 * count]))
        refs = refs[2 * count :]
    acc_ref = None
    if has_acc:
        acc_ref, _ = refs.pop(0), refs.pop(0)
    slot_refs = [refs.pop(0) for _ in range(5)] if final else None
    out_ref, note_ref = refs.pop(0), refs.pop(0)
    gu_ref, down_ref, sems = refs.pop(0), refs.pop(0), refs.pop(0)

    blocks = x_ref.shape[0] // ROWS
    width = x_ref.shape[1]
    step = 512
    contract = (((1,), (1,)), ((), ()))
    row = lax.broadcasted_iota(jnp.int32, (blocks, ROWS - FWD_AT, 1), 1) + FWD_AT
    is_fwd = (row >= CAP) & (row < 2 * CAP)

    fetches = []
    for number, pair in enumerate(sources):
        group = []
        for side, (pieces, held) in enumerate(zip(pair, (gu_ref, down_ref))):
            for k, ref in enumerate(pieces):
                into = held.at[number, pl.ds(k * ref.shape[0], ref.shape[0]), :]
                group.append(pltpu.make_async_copy(ref, into, sems.at[number, side, k]))
        fetches.append(group)
        for copy in group:
            copy.start()

    for number, group in enumerate(fetches):
        for copy in group:
            copy.wait()
        down = down_ref[number]
        gu_out = jnp.dot(x_ref[...], gu_ref[number], preferred_element_type=F32)
        half = gu_out.shape[1] // 2
        hidden_grad = lax.dot_general(c_ref[...], down, contract, preferred_element_type=F32)
        gate = gu_out[:, :half].reshape(blocks, ROWS, half)
        upper = gu_out[:, half:].reshape(blocks, ROWS, half)
        gate_f, up_f = gate[:, FWD_AT:], upper[:, FWD_AT:]
        hidden = gate_f / (1.0 + jnp.exp(-gate_f)) * up_f
        hidden = jnp.where(is_fwd, hidden, 0.0)
        hidden = hidden.reshape(blocks * (ROWS - FWD_AT), half).astype(BF16)
        gate_b = gate[:, :COT_ROWS].reshape(blocks * COT_ROWS, half)
        up_b = upper[:, :COT_ROWS].reshape(blocks * COT_ROWS, half)
        sig = 1.0 / (1.0 + jnp.exp(-gate_b))
        gate_grad = hidden_grad * up_b * sig * (1.0 + gate_b * (1.0 - sig))
        up_grad = hidden_grad * (gate_b * sig)
        grads = jnp.concatenate([gate_grad.astype(BF16), up_grad.astype(BF16)], axis=1)
        first = number == 0 and not has_acc
        for n in range(width // step):
            cols = slice(n * step, (n + 1) * step)
            back = lax.dot_general(grads, gu_ref[number, cols, :], contract, preferred_element_type=F32)
            fwd = jnp.dot(hidden, down_ref[number, :, cols], preferred_element_type=F32)
            back = back.reshape(blocks, COT_ROWS, step)
            fwd = fwd.reshape(blocks, ROWS - FWD_AT, step)
            pieces = [
                back[:, :FWD_AT],
                back[:, FWD_AT:] + fwd[:, : COT_ROWS - FWD_AT],
                fwd[:, COT_ROWS - FWD_AT :],
            ]
            value = jnp.concatenate(pieces, axis=1).reshape(blocks * ROWS, step)
            if not first:
                source = acc_ref if number == 0 else out_ref
                value = value + source[:, cols]
            out_ref[:, cols] = value.astype(out_ref.dtype)

    if final:
        weighing_ref, gain_ref, slot_in_ref, scale_ref, cot_ref = slot_refs
        both = jnp.dot(weighing_ref[...], out_ref[...], preferred_element_type=F32)
        count = weighing_ref.shape[0] // 2
        slot_q = (both[:count] + both[count:]) * gain_ref[...]
        slot_in = slot_in_ref[...]
        scale = scale_ref[...]
        inner = jnp.mean(slot_in * slot_q, axis=1, keepdims=True)
        note_ref[...] = cot_ref[...] + scale * slot_q - slot_in * (scale * scale * scale * inner)
    else:
        note_ref[...] = jnp.zeros_like(note_ref)


def expert_step(rows, cots, shards, before=None, slot_data=None):
    final = slot_data is not None
    parts = tuple(len(gu) for gu, _ in shards)
    operands = [rows, cots]
    for gu, d in shards:
        operands += list(gu) + list(d)
    near = pl.BlockSpec(memory_space=pltpu.VMEM)
    specs = [near, near] + [pl.BlockSpec(memory_space=pl.ANY)] * (len(operands) - 2)
    if before is not None:
        operands += list(before)
        specs += [near, near]
    if final:
        operands += list(slot_data)
        specs += [near] * len(slot_data)
    shape = rows.shape
    gu_shape = (sum(g.shape[0] for g in shards[0][0]), shards[0][0][0].shape[1])
    d_shape = (sum(d.shape[0] for d in shards[0][1]), shape[1])
    hidden = len(shards) * d_shape[0]
    cost = pl.CostEstimate(
        flops=2 * hidden * shape[1] * (2 * shape[0] + 4 * cots.shape[0]),
        transcendentals=hidden * 2 * cots.shape[0],
        bytes_accessed=sum(o.size * o.dtype.itemsize for o in operands) + 4 * rows.size,
    )
    note = (SLOTS if final else 8, shape[1] if final else 128)
    return pl.pallas_call(
        functools.partial(expert_kernel, parts, before is not None, final),
        out_shape=(jax.ShapeDtypeStruct(shape, BF16 if final else F32), jax.ShapeDtypeStruct(note, F32)),
        in_specs=specs,
        out_specs=(near, near),
        scratch_shapes=[
            pltpu.VMEM((len(shards), *gu_shape), BF16),
            pltpu.VMEM((len(shards), *d_shape), BF16),
            pltpu.SemaphoreType.DMA((len(shards), 2, max(parts))),
        ],
        compiler_params=pltpu.CompilerParams(vmem_limit_bytes=32 * 1024 * 1024),
        cost_estimate=cost,
    )(*operands)


def rotated(value, axis, distance):
    size = lax.axis_size(axis)
    return lax.ppermute(value, axis, [(i, (i + distance) % size) for i in range(size)])


def shifted(block, axis, distance):
    size = lax.axis_size(axis)
    route = [(i, i + distance) for i in range(size) if 0 <= i + distance < size]
    return lax.ppermute(block, axis, route)


def summed(value, axis):
    size = lax.axis_size(axis)
    distance = 1
    while distance < size:
        other = lax.ppermute(value.astype(BF16), axis, [(i, i ^ distance) for i in range(size)])
        value = value.astype(BF16).astype(F32) + other.astype(F32)
        distance *= 2
    return value


def on_device(
    fwd_acts,
    fwd_routes,
    fwd_weights,
    fwd_lengths,
    fwd_tenants,
    bwd_acts,
    bwd_routes,
    bwd_weights,
    bwd_lengths,
    bwd_tenants,
    bwd_cotangent,
    prompts,
    norm_gain,
    w_gate,
    w_up,
    w_down,
):
    tok_count, width = fwd_acts.shape[1:]
    gain_row = norm_gain[0]
    flat_table = prompts[0].reshape(SLOTS, width)

    own_gu = jnp.concatenate([w_gate[0, 0], w_up[0, 0]], axis=1)
    own_d = w_down[0, 0]
    gu_ring, d_ring = [(own_gu, own_gu)], [(own_d, own_d)]

    def onward(ring):
        up, down = ring[-1]
        ring.append((rotated(up, "split", 1), rotated(down, "split", -1)))

    def held_back(ring, note):
        up, down, note = lax.optimization_barrier((*ring[-1], note))
        ring[-1] = (up, down)
        return note

    def shards(step):
        return [((gu_ring[step][k],), (d_ring[step][k],)) for k in range(2)]

    for _ in range(2):
        onward(gu_ring)
        onward(d_ring)
    onward(gu_ring)

    first_row = (lax.axis_index("split") * lax.axis_size("column") + lax.axis_index("column")) * tok_count
    fwd_in, _, fwd_normed, _, _, _ = prepare(
        fwd_acts[0], fwd_lengths[0], fwd_tenants[0], flat_table, gain_row, first_row
    )
    bwd_in, bwd_scale, bwd_normed, bwd_slot, slot, selector = prepare(
        bwd_acts[0], bwd_lengths[0], bwd_tenants[0], flat_table, gain_row, first_row
    )
    cotangent = bwd_cotangent[0]
    f_route, b_route = fwd_routes[0, :, 0], bwd_routes[0, :, 0]
    f_rank, b_rank = ranks(f_route), ranks(b_route)
    weight_b = bwd_weights[0, :, 0]
    high = lax.reduce_precision(weight_b, 8, 7)
    low = weight_b - high
    lane = jnp.arange(EXTRA, dtype=jnp.int32)[None, :]
    extra = jnp.where(lane == 0, high[:, None], 0.0)
    extra = jnp.where(lane == 1, low[:, None], extra)
    extra = jnp.where(lane == 2, slot.astype(F32)[:, None], extra).astype(BF16)
    blank = jnp.zeros((tok_count, EXTRA), BF16)
    sources = jnp.concatenate(
        [
            jnp.concatenate([bwd_normed, extra], axis=1),
            jnp.concatenate([fwd_normed, blank], axis=1),
            jnp.concatenate([cotangent, blank], axis=1),
        ],
        axis=0,
    )
    target = jnp.concatenate(
        [
            b_route * BLOCK + b_rank,
            f_route * BLOCK + CAP + f_rank,
            b_route * BLOCK + ROWS + b_rank,
        ]
    )
    picker = target[None, :] == jnp.arange(EXPERTS * BLOCK, dtype=jnp.int32)[:, None]
    packed = jnp.dot(picker.astype(BF16), sources, preferred_element_type=F32).astype(BF16)
    packed = packed.reshape(EXPERTS, BLOCK, width + EXTRA)
    packed, _ = lax.optimization_barrier((packed, gu_ring[1]))
    arrived = lax.all_to_all(packed, "column", split_axis=0, concat_axis=0, tiled=True)
    rows = arrived[:, :ROWS, :width].reshape(EXPERTS * ROWS, width)
    cots = arrived[:, ROWS:, :width].reshape(EXPERTS * COT_ROWS, width)
    notes = arrived[:, :ROWS, width : width + 3].astype(F32).reshape(EXPERTS * ROWS, 3)

    at_slot = notes[:, 2][None, :] == jnp.arange(SLOTS, dtype=F32)[:, None]
    weighing = jnp.concatenate(
        [jnp.where(at_slot, notes[:, 0][None, :], 0.0), jnp.where(at_slot, notes[:, 1][None, :], 0.0)], axis=0
    ).astype(BF16)
    slot_in = flat_table.astype(F32)
    slot_scale = lax.rsqrt(jnp.mean(slot_in * slot_in, axis=1, keepdims=True) + EPS)
    slot_cot = jnp.dot(jnp.transpose(selector.astype(BF16)), cotangent, preferred_element_type=F32)
    slot_data = (weighing, norm_gain, slot_in, slot_scale, slot_cot)

    acc, note = expert_step(rows, cots, [((own_gu,), (own_d,))] + shards(1))
    note = held_back(d_ring, note)
    onward(d_ring)
    acc, note = expert_step(rows, cots, shards(2), (acc, note))
    note = held_back(d_ring, note)
    gu_up, gu_down = gu_ring[-1]
    d_up, d_down = d_ring[-1]
    half_k, half_h = width // 2, own_d.shape[0] // 2
    last = (
        (rotated(gu_up[:half_k], "split", 1), rotated(gu_down[half_k:], "split", -1)),
        (rotated(d_up[:half_h], "split", 1), rotated(d_down[half_h:], "split", -1)),
    )
    before = expert_step(rows, cots, shards(3), (acc, note))
    partial, local_sums = expert_step(rows, cots, [last], before, slot_data)

    returned = lax.all_to_all(
        partial.reshape(EXPERTS, ROWS, width), "column", split_axis=0, concat_axis=0, tiled=True
    ).reshape(EXPERTS * ROWS, width)
    totals = summed(summed(local_sums, "split"), "column")
    prompt_grads = totals.astype(BF16).reshape(1, TENANTS, PLEN, width)

    home = jnp.arange(EXPERTS * ROWS, dtype=jnp.int32)[None, :]
    f_take = ((f_route * ROWS + CAP + f_rank)[:, None] == home).astype(BF16)
    b_take = ((b_route * ROWS + b_rank)[:, None] == home).astype(BF16)
    f_out = jnp.dot(f_take, returned, preferred_element_type=F32)
    leaving = (fwd_in.astype(F32) + fwd_weights[0] * f_out).astype(BF16)
    next_acts = shifted(leaving, "phase", 1)
    back_out = jnp.dot(b_take, returned, preferred_element_type=F32)
    scaled = bwd_weights[0] * back_out * gain_row[None, :]
    wide = bwd_in.astype(F32)
    inner = jnp.mean(wide * scaled, axis=1, keepdims=True)
    input_grad = cotangent.astype(F32) + bwd_scale * scaled - wide * bwd_scale**3 * inner
    to_prev = jnp.where(bwd_slot[:, None], 0.0, input_grad).astype(BF16)
    prev_grads = shifted(to_prev, "phase", -1)
    return next_acts[None], prev_grads[None], prompt_grads


def solution(mesh):
    names = mesh.axis_names
    phases, experts = mesh.shape[names[0]], mesh.shape[names[1]]
    grid = mesh.devices.reshape(phases, experts // EXPERTS, EXPERTS)
    inner = Mesh(grid, ("phase", "split", "column"))
    both = ("split", "column")
    tokens = P("phase", both, None)
    per_phase = P("phase", None)
    weights = P("phase", both, None, None)
    table = P("phase", None, None, None)
    placed = (
        tokens,
        tokens,
        tokens,
        per_phase,
        per_phase,
        tokens,
        tokens,
        tokens,
        per_phase,
        per_phase,
        tokens,
        table,
        per_phase,
        weights,
        weights,
        weights,
    )
    return jax.shard_map(
        on_device,
        mesh=inner,
        in_specs=placed,
        out_specs=(tokens, tokens, table),
        check_vma=False,
    )
```

```python
import functools

import jax
import jax.numpy as jnp
from jax import lax
from jax.experimental import pallas as pl
from jax.experimental.pallas import tpu as pltpu
from jax.sharding import Mesh, PartitionSpec as P

EXPERTS = 8
TENANTS = 2
PLEN = 10
SLOTS = TENANTS * PLEN
CAP = 18
ROWS = 40
COT_ROWS = 24
BLOCK = ROWS + COT_ROWS
FWD_AT = 16
EXTRA = 128
NO_SLOT = 31
LOW_AT = 32
VMEM_MIB = 18

EPS = 1e-06
BF16 = jnp.bfloat16
F32 = jnp.float32


def token_layout(lengths, tenants, first_row, tok_count):
    count = lengths.shape[0]
    token_index = first_row + jnp.arange(tok_count, dtype=jnp.int32)
    order = jnp.arange(count, dtype=jnp.int32)
    earlier = order[:, None] < order[None, :]
    seg_starts = jnp.sum(jnp.where(earlier, lengths[:, None], 0), axis=0)
    seg_ends = seg_starts + lengths
    chosen = (seg_starts[None, :] <= token_index[:, None]) & (token_index[:, None] < seg_ends[None, :])
    position = token_index - jnp.sum(jnp.where(chosen, seg_starts[None, :], 0), axis=1)
    tenant = jnp.sum(jnp.where(chosen, tenants[None, :], 0), axis=1)
    return position, tenant


def prepare(acts, lengths, tenants, flat_table, gain_row, first_row):
    tok_count = acts.shape[0]
    position, tenant = token_layout(lengths, tenants, first_row, tok_count)
    prompt_slot = position < PLEN
    slot = jnp.where(prompt_slot, tenant * PLEN + position, NO_SLOT)
    selector = slot[:, None] == jnp.arange(SLOTS, dtype=jnp.int32)[None, :]
    prompt_rows = jnp.dot(selector.astype(BF16), flat_table, preferred_element_type=F32).astype(BF16)
    inputs = jnp.where(prompt_slot[:, None], prompt_rows, acts)
    widened = inputs.astype(F32)
    inv_scale = lax.rsqrt(jnp.mean(widened * widened, axis=1, keepdims=True) + EPS)
    normed = (widened * inv_scale * gain_row[None, :]).astype(BF16)
    return inputs, inv_scale, normed, prompt_slot, slot, selector


def ranks(routes):
    tok_count = routes.shape[0]
    at = jnp.arange(tok_count, dtype=jnp.int32)
    same = (routes[None, :] == routes[:, None]) & (at[None, :] < at[:, None])
    return jnp.sum(same.astype(jnp.int32), axis=1)


def expert_kernel(parts, has_acc, final, *refs):
    refs = list(refs)
    x_ref, c_ref = refs.pop(0), refs.pop(0)
    sources = []
    for count in parts:
        sources.append((refs[:count], refs[count : 2 * count]))
        refs = refs[2 * count :]
    acc_ref = None
    if has_acc:
        acc_ref, _ = refs.pop(0), refs.pop(0)
    slot_refs = [refs.pop(0) for _ in range(4)] if final else None
    out_ref, note_ref = refs.pop(0), refs.pop(0)
    gu_ref, down_ref, sems = refs.pop(0), refs.pop(0), refs.pop(0)

    blocks = x_ref.shape[0] // ROWS
    width = c_ref.shape[1]
    step = 512
    contract = (((1,), (1,)), ((), ()))
    row = lax.broadcasted_iota(jnp.int32, (blocks, ROWS - FWD_AT, 1), 1) + FWD_AT
    is_fwd = (row >= CAP) & (row < 2 * CAP)

    fetches = []
    for number, pair in enumerate(sources):
        group = []
        for side, (pieces, held) in enumerate(zip(pair, (gu_ref, down_ref))):
            for k, ref in enumerate(pieces):
                into = held.at[number, pl.ds(k * ref.shape[0], ref.shape[0]), :]
                group.append(pltpu.make_async_copy(ref, into, sems.at[number, side, k]))
        fetches.append(group)
        for copy in group:
            copy.start()

    for number, group in enumerate(fetches):
        for copy in group:
            copy.wait()
        down = down_ref[number]
        gu_out = jnp.dot(x_ref[:, :width], gu_ref[number], preferred_element_type=F32)
        half = gu_out.shape[1] // 2
        hidden_grad = lax.dot_general(c_ref[...], down, contract, preferred_element_type=F32)
        gate = gu_out[:, :half].reshape(blocks, ROWS, half)
        upper = gu_out[:, half:].reshape(blocks, ROWS, half)
        gate_f, up_f = gate[:, FWD_AT:], upper[:, FWD_AT:]
        hidden = gate_f / (1.0 + jnp.exp(-gate_f)) * up_f
        hidden = jnp.where(is_fwd, hidden, 0.0)
        hidden = hidden.reshape(blocks * (ROWS - FWD_AT), half).astype(BF16)
        gate_b = gate[:, :COT_ROWS].reshape(blocks * COT_ROWS, half)
        up_b = upper[:, :COT_ROWS].reshape(blocks * COT_ROWS, half)
        sig = 1.0 / (1.0 + jnp.exp(-gate_b))
        gate_grad = hidden_grad * up_b * sig * (1.0 + gate_b * (1.0 - sig))
        up_grad = hidden_grad * (gate_b * sig)
        grads = jnp.concatenate([gate_grad.astype(BF16), up_grad.astype(BF16)], axis=1)
        first = number == 0 and not has_acc
        for n in range(width // step):
            cols = slice(n * step, (n + 1) * step)
            back = lax.dot_general(grads, gu_ref[number, cols, :], contract, preferred_element_type=F32)
            fwd = jnp.dot(hidden, down_ref[number, :, cols], preferred_element_type=F32)
            back = back.reshape(blocks, COT_ROWS, step)
            fwd = fwd.reshape(blocks, ROWS - FWD_AT, step)
            pieces = [
                back[:, :FWD_AT],
                back[:, FWD_AT:] + fwd[:, : COT_ROWS - FWD_AT],
                fwd[:, COT_ROWS - FWD_AT :],
            ]
            value = jnp.concatenate(pieces, axis=1).reshape(blocks * ROWS, step)
            if not first:
                source = acc_ref if number == 0 else out_ref
                value = value + source[:, cols]
            out_ref[:, cols] = value.astype(out_ref.dtype)

    if final:
        gain_ref, slot_in_ref, scale_ref, cot_ref = slot_refs
        count = slot_in_ref.shape[0]
        notes = x_ref[:, width:].astype(F32)
        lane = lax.broadcasted_iota(jnp.int32, notes.shape, 1).astype(F32)
        high = jnp.where(lane == notes[:, 2:3], notes[:, 0:1], 0.0)
        low = jnp.where(lane - LOW_AT == notes[:, 2:3], notes[:, 1:2], 0.0)
        weighing = jnp.where(lane < LOW_AT, high, low).astype(BF16)
        both = lax.dot_general(
            weighing, out_ref[...], (((0,), (0,)), ((), ())), preferred_element_type=F32
        )
        slot_q = (both[:count] + both[LOW_AT : LOW_AT + count]) * gain_ref[...]
        slot_in = slot_in_ref[...]
        scale = scale_ref[...]
        inner = jnp.mean(slot_in * slot_q, axis=1, keepdims=True)
        note_ref[...] = cot_ref[...] + scale * slot_q - slot_in * (scale * scale * scale * inner)
    else:
        note_ref[...] = jnp.zeros_like(note_ref)


def expert_step(rows, cots, shards, before=None, slot_data=None):
    final = slot_data is not None
    parts = tuple(len(gu) for gu, _ in shards)
    operands = [rows, cots]
    for gu, d in shards:
        operands += list(gu) + list(d)
    near = pl.BlockSpec(memory_space=pltpu.VMEM)
    specs = [near, near] + [pl.BlockSpec(memory_space=pl.ANY)] * (len(operands) - 2)
    if before is not None:
        operands += list(before)
        specs += [near, near]
    if final:
        operands += list(slot_data)
        specs += [near] * len(slot_data)
    shape = (rows.shape[0], cots.shape[1])
    gu_shape = (sum(g.shape[0] for g in shards[0][0]), shards[0][0][0].shape[1])
    d_shape = (sum(d.shape[0] for d in shards[0][1]), shape[1])
    hidden = len(shards) * d_shape[0]
    cost = pl.CostEstimate(
        flops=2 * hidden * shape[1] * (2 * shape[0] + 4 * cots.shape[0]),
        transcendentals=hidden * 2 * cots.shape[0],
        bytes_accessed=sum(o.size * o.dtype.itemsize for o in operands) + 4 * shape[0] * shape[1],
    )
    note = (SLOTS if final else 8, shape[1] if final else 128)
    return pl.pallas_call(
        functools.partial(expert_kernel, parts, before is not None, final),
        out_shape=(jax.ShapeDtypeStruct(shape, BF16 if final else F32), jax.ShapeDtypeStruct(note, F32)),
        in_specs=specs,
        out_specs=(near, near),
        scratch_shapes=[
            pltpu.VMEM((len(shards), *gu_shape), BF16),
            pltpu.VMEM((len(shards), *d_shape), BF16),
            pltpu.SemaphoreType.DMA((len(shards), 2, max(parts))),
        ],
        compiler_params=pltpu.CompilerParams(vmem_limit_bytes=VMEM_MIB * 1024 * 1024),
        cost_estimate=cost,
    )(*operands)


def rotated(value, axis, distance):
    size = lax.axis_size(axis)
    return lax.ppermute(value, axis, [(i, (i + distance) % size) for i in range(size)])


def shifted(block, axis, distance):
    size = lax.axis_size(axis)
    route = [(i, i + distance) for i in range(size) if 0 <= i + distance < size]
    return lax.ppermute(block, axis, route)


def summed(value, axis):
    size = lax.axis_size(axis)
    distance = 1
    while distance < size:
        other = lax.ppermute(value.astype(BF16), axis, [(i, i ^ distance) for i in range(size)])
        value = value.astype(BF16).astype(F32) + other.astype(F32)
        distance *= 2
    return value


def on_device(
    fwd_acts,
    fwd_routes,
    fwd_weights,
    fwd_lengths,
    fwd_tenants,
    bwd_acts,
    bwd_routes,
    bwd_weights,
    bwd_lengths,
    bwd_tenants,
    bwd_cotangent,
    prompts,
    norm_gain,
    w_gate,
    w_up,
    w_down,
):
    tok_count, width = fwd_acts.shape[1:]
    gain_row = norm_gain[0]
    flat_table = prompts[0].reshape(SLOTS, width)

    own_gu = jnp.concatenate([w_gate[0, 0], w_up[0, 0]], axis=1)
    own_d = w_down[0, 0]
    gu_ring, d_ring = [(own_gu, own_gu)], [(own_d, own_d)]

    def onward(ring):
        up, down = ring[-1]
        ring.append((rotated(up, "split", 1), rotated(down, "split", -1)))

    def held_back(ring, note):
        up, down, note = lax.optimization_barrier((*ring[-1], note))
        ring[-1] = (up, down)
        return note

    def shards(step):
        return [((gu_ring[step][k],), (d_ring[step][k],)) for k in range(2)]

    for _ in range(2):
        onward(gu_ring)
        onward(d_ring)
    onward(gu_ring)

    first_row = (lax.axis_index("split") * lax.axis_size("column") + lax.axis_index("column")) * tok_count
    fwd_in, _, fwd_normed, _, _, _ = prepare(
        fwd_acts[0], fwd_lengths[0], fwd_tenants[0], flat_table, gain_row, first_row
    )
    bwd_in, bwd_scale, bwd_normed, bwd_slot, slot, selector = prepare(
        bwd_acts[0], bwd_lengths[0], bwd_tenants[0], flat_table, gain_row, first_row
    )
    cotangent = bwd_cotangent[0]
    f_route, b_route = fwd_routes[0, :, 0], bwd_routes[0, :, 0]
    f_rank, b_rank = ranks(f_route), ranks(b_route)
    weight_b = bwd_weights[0, :, 0]
    high = lax.reduce_precision(weight_b, 8, 7)
    low = weight_b - high
    lane = jnp.arange(EXTRA, dtype=jnp.int32)[None, :]
    extra = jnp.where(lane == 0, high[:, None], 0.0)
    extra = jnp.where(lane == 1, low[:, None], extra)
    extra = jnp.where(lane == 2, slot.astype(F32)[:, None], extra).astype(BF16)
    blank = jnp.zeros((tok_count, EXTRA), BF16)
    sources = jnp.concatenate(
        [
            jnp.concatenate([bwd_normed, extra], axis=1),
            jnp.concatenate([fwd_normed, blank], axis=1),
            jnp.concatenate([cotangent, blank], axis=1),
        ],
        axis=0,
    )
    target = jnp.concatenate(
        [
            b_route * BLOCK + b_rank,
            f_route * BLOCK + CAP + f_rank,
            b_route * BLOCK + ROWS + b_rank,
        ]
    )
    picker = target[None, :] == jnp.arange(EXPERTS * BLOCK, dtype=jnp.int32)[:, None]
    packed = jnp.dot(picker.astype(BF16), sources, preferred_element_type=F32).astype(BF16)
    packed = packed.reshape(EXPERTS, BLOCK, width + EXTRA)
    packed, _ = lax.optimization_barrier((packed, gu_ring[1]))
    arrived = lax.all_to_all(packed, "column", split_axis=0, concat_axis=0, tiled=True)
    rows = arrived[:, :ROWS].reshape(EXPERTS * ROWS, width + EXTRA)
    cots = arrived[:, ROWS:, :width].reshape(EXPERTS * COT_ROWS, width)

    slot_in = flat_table.astype(F32)
    slot_scale = lax.rsqrt(jnp.mean(slot_in * slot_in, axis=1, keepdims=True) + EPS)
    slot_cot = jnp.dot(jnp.transpose(selector.astype(BF16)), cotangent, preferred_element_type=F32)
    slot_data = (norm_gain, slot_in, slot_scale, slot_cot)

    acc, note = expert_step(rows, cots, [((own_gu,), (own_d,))] + shards(1))
    note = held_back(d_ring, note)
    onward(d_ring)
    acc, note = expert_step(rows, cots, shards(2), (acc, note))
    note = held_back(d_ring, note)
    last = ((rotated(gu_ring[-1][0], "split", 1),), (rotated(d_ring[-1][1], "split", -1),))
    before = expert_step(rows, cots, shards(3), (acc, note))
    partial, local_sums = expert_step(rows, cots, [last], before, slot_data)

    returned = lax.all_to_all(
        partial.reshape(EXPERTS, ROWS, width), "column", split_axis=0, concat_axis=0, tiled=True
    ).reshape(EXPERTS * ROWS, width)
    totals = summed(summed(local_sums, "split"), "column")
    prompt_grads = totals.astype(BF16).reshape(1, TENANTS, PLEN, width)

    home = jnp.arange(EXPERTS * ROWS, dtype=jnp.int32)[None, :]
    f_take = ((f_route * ROWS + CAP + f_rank)[:, None] == home).astype(BF16)
    b_take = ((b_route * ROWS + b_rank)[:, None] == home).astype(BF16)
    f_out = jnp.dot(f_take, returned, preferred_element_type=F32)
    leaving = (fwd_in.astype(F32) + fwd_weights[0] * f_out).astype(BF16)
    next_acts = shifted(leaving, "phase", 1)
    back_out = jnp.dot(b_take, returned, preferred_element_type=F32)
    scaled = bwd_weights[0] * back_out * gain_row[None, :]
    wide = bwd_in.astype(F32)
    inner = jnp.mean(wide * scaled, axis=1, keepdims=True)
    input_grad = cotangent.astype(F32) + bwd_scale * scaled - wide * bwd_scale**3 * inner
    to_prev = jnp.where(bwd_slot[:, None], 0.0, input_grad).astype(BF16)
    prev_grads = shifted(to_prev, "phase", -1)
    return next_acts[None], prev_grads[None], prompt_grads


def solution(mesh):
    names = mesh.axis_names
    phases, experts = mesh.shape[names[0]], mesh.shape[names[1]]
    grid = mesh.devices.reshape(phases, experts // EXPERTS, EXPERTS)
    inner = Mesh(grid, ("phase", "split", "column"))
    both = ("split", "column")
    tokens = P("phase", both, None)
    per_phase = P("phase", None)
    weights = P("phase", both, None, None)
    table = P("phase", None, None, None)
    placed = (
        tokens,
        tokens,
        tokens,
        per_phase,
        per_phase,
        tokens,
        tokens,
        tokens,
        per_phase,
        per_phase,
        tokens,
        table,
        per_phase,
        weights,
        weights,
        weights,
    )
    return jax.shard_map(
        on_device,
        mesh=inner,
        in_specs=placed,
        out_specs=(tokens, tokens, table),
        check_vma=False,
    )
```

```python
import functools

import jax
import jax.numpy as jnp
from jax import lax
from jax.experimental import pallas as pl
from jax.experimental.pallas import tpu as pltpu
from jax.sharding import Mesh, PartitionSpec as P

EXPERTS = 8
TENANTS = 2
PLEN = 10
SLOTS = TENANTS * PLEN
CAP = 18
ROWS = 40
COT_ROWS = 24
BLOCK = ROWS + COT_ROWS
FWD_AT = 16
EXTRA = 128
NO_SLOT = 31
LOW_AT = 32
VMEM_MIB = 18
SHARD_SPACE = pltpu.HBM

EPS = 1e-06
BF16 = jnp.bfloat16
F32 = jnp.float32


def token_layout(lengths, tenants, first_row, tok_count):
    count = lengths.shape[0]
    token_index = first_row + jnp.arange(tok_count, dtype=jnp.int32)
    order = jnp.arange(count, dtype=jnp.int32)
    earlier = order[:, None] < order[None, :]
    seg_starts = jnp.sum(jnp.where(earlier, lengths[:, None], 0), axis=0)
    seg_ends = seg_starts + lengths
    chosen = (seg_starts[None, :] <= token_index[:, None]) & (token_index[:, None] < seg_ends[None, :])
    position = token_index - jnp.sum(jnp.where(chosen, seg_starts[None, :], 0), axis=1)
    tenant = jnp.sum(jnp.where(chosen, tenants[None, :], 0), axis=1)
    return position, tenant


def prepare(acts, lengths, tenants, flat_table, gain_row, first_row):
    tok_count = acts.shape[0]
    position, tenant = token_layout(lengths, tenants, first_row, tok_count)
    prompt_slot = position < PLEN
    slot = jnp.where(prompt_slot, tenant * PLEN + position, NO_SLOT)
    selector = slot[:, None] == jnp.arange(SLOTS, dtype=jnp.int32)[None, :]
    prompt_rows = jnp.dot(selector.astype(BF16), flat_table, preferred_element_type=F32).astype(BF16)
    inputs = jnp.where(prompt_slot[:, None], prompt_rows, acts)
    widened = inputs.astype(F32)
    inv_scale = lax.rsqrt(jnp.mean(widened * widened, axis=1, keepdims=True) + EPS)
    normed = (widened * inv_scale * gain_row[None, :]).astype(BF16)
    return inputs, inv_scale, normed, prompt_slot, slot, selector


def ranks(routes):
    tok_count = routes.shape[0]
    at = jnp.arange(tok_count, dtype=jnp.int32)
    same = (routes[None, :] == routes[:, None]) & (at[None, :] < at[:, None])
    return jnp.sum(same.astype(jnp.int32), axis=1)


def shard_kernel(gate_ref, up_ref, down_ref, front_ref, rest_ref):
    width, half = gate_ref.shape
    cut = front_ref.shape[0]
    front_ref[:, :half] = gate_ref[:cut, :]
    front_ref[:, half:] = up_ref[:cut, :]
    rest_ref[: width - cut, :half] = gate_ref[cut:, :]
    rest_ref[: width - cut, half:] = up_ref[cut:, :]
    for k in range(width // (2 * half)):
        rows = slice(width - cut + k * half, width - cut + (k + 1) * half)
        rest_ref[rows, :] = down_ref[:, 2 * half * k : 2 * half * (k + 1)]


def shard_arrays(gate, upper, down):
    width, half = gate.shape
    cut = 3 * width // 4
    near = pl.BlockSpec(memory_space=pltpu.VMEM)
    shape = jax.ShapeDtypeStruct((cut, 2 * half), BF16)
    return pl.pallas_call(
        shard_kernel,
        out_shape=(shape, shape),
        in_specs=[near] * 3,
        out_specs=(near, near),
        compiler_params=pltpu.CompilerParams(vmem_limit_bytes=VMEM_MIB * 1024 * 1024),
    )(gate, upper, down)


def expert_kernel(count, has_acc, final, *refs):
    refs = list(refs)
    x_ref, c_ref = refs.pop(0), refs.pop(0)
    sources = [(refs.pop(0), refs.pop(0)) for _ in range(count)]
    acc_ref = None
    if has_acc:
        acc_ref, _ = refs.pop(0), refs.pop(0)
    slot_refs = [refs.pop(0) for _ in range(4)] if final else None
    out_ref, note_ref = refs.pop(0), refs.pop(0)
    gu_ref, down_ref, sems = refs.pop(0), refs.pop(0), refs.pop(0)

    blocks = x_ref.shape[0] // ROWS
    width = c_ref.shape[1]
    step = 512
    contract = (((1,), (1,)), ((), ()))
    row = lax.broadcasted_iota(jnp.int32, (blocks, ROWS - FWD_AT, 1), 1) + FWD_AT
    is_fwd = (row >= CAP) & (row < 2 * CAP)

    fetches = []
    for number, (front, rest) in enumerate(sources):
        cut = front.shape[0]
        group = [
            pltpu.make_async_copy(front, gu_ref.at[number, pl.ds(0, cut), :], sems.at[number, 0]),
            pltpu.make_async_copy(
                rest.at[pl.ds(0, width - cut), :],
                gu_ref.at[number, pl.ds(cut, width - cut), :],
                sems.at[number, 1],
            ),
            pltpu.make_async_copy(
                rest.at[pl.ds(width - cut, down_ref.shape[1]), :], down_ref.at[number], sems.at[number, 2]
            ),
        ]
        fetches.append(group)
        for copy in group:
            copy.start()

    folds = width // gu_ref.shape[2]
    deep = down_ref.shape[1] // folds
    for number, group in enumerate(fetches):
        for copy in group:
            copy.wait()
        down = jnp.concatenate(
            [down_ref[number, k * deep : (k + 1) * deep, :] for k in range(folds)], axis=1
        )
        gu_out = jnp.dot(x_ref[:, :width], gu_ref[number], preferred_element_type=F32)
        half = gu_out.shape[1] // 2
        hidden_grad = lax.dot_general(c_ref[...], down, contract, preferred_element_type=F32)
        gate = gu_out[:, :half].reshape(blocks, ROWS, half)
        upper = gu_out[:, half:].reshape(blocks, ROWS, half)
        gate_f, up_f = gate[:, FWD_AT:], upper[:, FWD_AT:]
        hidden = gate_f / (1.0 + jnp.exp(-gate_f)) * up_f
        hidden = jnp.where(is_fwd, hidden, 0.0)
        hidden = hidden.reshape(blocks * (ROWS - FWD_AT), half).astype(BF16)
        gate_b = gate[:, :COT_ROWS].reshape(blocks * COT_ROWS, half)
        up_b = upper[:, :COT_ROWS].reshape(blocks * COT_ROWS, half)
        sig = 1.0 / (1.0 + jnp.exp(-gate_b))
        gate_grad = hidden_grad * up_b * sig * (1.0 + gate_b * (1.0 - sig))
        up_grad = hidden_grad * (gate_b * sig)
        grads = jnp.concatenate([gate_grad.astype(BF16), up_grad.astype(BF16)], axis=1)
        first = number == 0 and not has_acc
        for n in range(width // step):
            cols = slice(n * step, (n + 1) * step)
            back = lax.dot_general(grads, gu_ref[number, cols, :], contract, preferred_element_type=F32)
            fwd = jnp.dot(hidden, down[:, cols], preferred_element_type=F32)
            back = back.reshape(blocks, COT_ROWS, step)
            fwd = fwd.reshape(blocks, ROWS - FWD_AT, step)
            pieces = [
                back[:, :FWD_AT],
                back[:, FWD_AT:] + fwd[:, : COT_ROWS - FWD_AT],
                fwd[:, COT_ROWS - FWD_AT :],
            ]
            value = jnp.concatenate(pieces, axis=1).reshape(blocks * ROWS, step)
            if not first:
                source = acc_ref if number == 0 else out_ref
                value = value + source[:, cols]
            out_ref[:, cols] = value.astype(out_ref.dtype)

    if final:
        gain_ref, slot_in_ref, scale_ref, cot_ref = slot_refs
        slots = slot_in_ref.shape[0]
        notes = x_ref[:, width:].astype(F32)
        lane = lax.broadcasted_iota(jnp.int32, notes.shape, 1).astype(F32)
        high = jnp.where(lane == notes[:, 2:3], notes[:, 0:1], 0.0)
        low = jnp.where(lane - LOW_AT == notes[:, 2:3], notes[:, 1:2], 0.0)
        weighing = jnp.where(lane < LOW_AT, high, low).astype(BF16)
        both = lax.dot_general(
            weighing, out_ref[...], (((0,), (0,)), ((), ())), preferred_element_type=F32
        )
        slot_q = (both[:slots] + both[LOW_AT : LOW_AT + slots]) * gain_ref[...]
        slot_in = slot_in_ref[...]
        scale = scale_ref[...]
        inner = jnp.mean(slot_in * slot_q, axis=1, keepdims=True)
        note_ref[...] = cot_ref[...] + scale * slot_q - slot_in * (scale * scale * scale * inner)
    else:
        note_ref[...] = jnp.zeros_like(note_ref)


def expert_step(rows, cots, shards, before=None, slot_data=None):
    final = slot_data is not None
    operands = [rows, cots]
    for pair in shards:
        operands += [pltpu.with_memory_space_constraint(part, pltpu.HBM) for part in pair]
    near = pl.BlockSpec(memory_space=pltpu.VMEM)
    specs = [near, near] + [pl.BlockSpec(memory_space=SHARD_SPACE)] * (len(operands) - 2)
    if before is not None:
        operands += list(before)
        specs += [near, near]
    if final:
        operands += list(slot_data)
        specs += [near] * len(slot_data)
    shape = (rows.shape[0], cots.shape[1])
    lanes = shards[0][0].shape[1]
    deep = shards[0][0].shape[0] + shards[0][1].shape[0] - shape[1]
    hidden = len(shards) * lanes // 2
    cost = pl.CostEstimate(
        flops=2 * hidden * shape[1] * (2 * shape[0] + 4 * cots.shape[0]),
        transcendentals=hidden * 2 * cots.shape[0],
        bytes_accessed=sum(o.size * o.dtype.itemsize for o in operands) + 4 * shape[0] * shape[1],
    )
    note = (SLOTS if final else 8, shape[1] if final else 128)
    return pl.pallas_call(
        functools.partial(expert_kernel, len(shards), before is not None, final),
        out_shape=(jax.ShapeDtypeStruct(shape, BF16 if final else F32), jax.ShapeDtypeStruct(note, F32)),
        in_specs=specs,
        out_specs=(near, near),
        scratch_shapes=[
            pltpu.VMEM((len(shards), shape[1], lanes), BF16),
            pltpu.VMEM((len(shards), deep, lanes), BF16),
            pltpu.SemaphoreType.DMA((len(shards), 3)),
        ],
        compiler_params=pltpu.CompilerParams(vmem_limit_bytes=VMEM_MIB * 1024 * 1024),
        cost_estimate=cost,
    )(*operands)


def rotated(value, axis, distance):
    size = lax.axis_size(axis)
    return lax.ppermute(value, axis, [(i, (i + distance) % size) for i in range(size)])


def shifted(block, axis, distance):
    size = lax.axis_size(axis)
    route = [(i, i + distance) for i in range(size) if 0 <= i + distance < size]
    return lax.ppermute(block, axis, route)


def summed(value, axis):
    size = lax.axis_size(axis)
    distance = 1
    while distance < size:
        other = lax.ppermute(value.astype(BF16), axis, [(i, i ^ distance) for i in range(size)])
        value = value.astype(BF16).astype(F32) + other.astype(F32)
        distance *= 2
    return value


def on_device(
    fwd_acts,
    fwd_routes,
    fwd_weights,
    fwd_lengths,
    fwd_tenants,
    bwd_acts,
    bwd_routes,
    bwd_weights,
    bwd_lengths,
    bwd_tenants,
    bwd_cotangent,
    prompts,
    norm_gain,
    w_gate,
    w_up,
    w_down,
):
    tok_count, width = fwd_acts.shape[1:]
    gain_row = norm_gain[0]
    flat_table = prompts[0].reshape(SLOTS, width)

    own_front, own_rest = shard_arrays(w_gate[0, 0], w_up[0, 0], w_down[0, 0])
    front_ring, rest_ring = [(own_front, own_front)], [(own_rest, own_rest)]

    def onward(ring):
        up, down = ring[-1]
        ring.append((rotated(up, "split", 1), rotated(down, "split", -1)))

    def held_back(ring, note):
        up, down, note = lax.optimization_barrier((*ring[-1], note))
        ring[-1] = (up, down)
        return note

    def shards(step):
        return [(front_ring[step][k], rest_ring[step][k]) for k in range(2)]

    for _ in range(2):
        onward(front_ring)
        onward(rest_ring)
    onward(front_ring)

    first_row = (lax.axis_index("split") * lax.axis_size("column") + lax.axis_index("column")) * tok_count
    fwd_in, _, fwd_normed, _, _, _ = prepare(
        fwd_acts[0], fwd_lengths[0], fwd_tenants[0], flat_table, gain_row, first_row
    )
    bwd_in, bwd_scale, bwd_normed, bwd_slot, slot, selector = prepare(
        bwd_acts[0], bwd_lengths[0], bwd_tenants[0], flat_table, gain_row, first_row
    )
    cotangent = bwd_cotangent[0]
    f_route, b_route = fwd_routes[0, :, 0], bwd_routes[0, :, 0]
    f_rank, b_rank = ranks(f_route), ranks(b_route)
    weight_b = bwd_weights[0, :, 0]
    high = lax.reduce_precision(weight_b, 8, 7)
    low = weight_b - high
    lane = jnp.arange(EXTRA, dtype=jnp.int32)[None, :]
    extra = jnp.where(lane == 0, high[:, None], 0.0)
    extra = jnp.where(lane == 1, low[:, None], extra)
    extra = jnp.where(lane == 2, slot.astype(F32)[:, None], extra).astype(BF16)
    blank = jnp.zeros((tok_count, EXTRA), BF16)
    sources = jnp.concatenate(
        [
            jnp.concatenate([bwd_normed, extra], axis=1),
            jnp.concatenate([fwd_normed, blank], axis=1),
            jnp.concatenate([cotangent, blank], axis=1),
        ],
        axis=0,
    )
    target = jnp.concatenate(
        [
            b_route * BLOCK + b_rank,
            f_route * BLOCK + CAP + f_rank,
            b_route * BLOCK + ROWS + b_rank,
        ]
    )
    picker = target[None, :] == jnp.arange(EXPERTS * BLOCK, dtype=jnp.int32)[:, None]
    packed = jnp.dot(picker.astype(BF16), sources, preferred_element_type=F32).astype(BF16)
    packed = packed.reshape(EXPERTS, BLOCK, width + EXTRA)
    packed, _ = lax.optimization_barrier((packed, front_ring[1]))
    arrived = lax.all_to_all(packed, "column", split_axis=0, concat_axis=0, tiled=True)
    rows = arrived[:, :ROWS].reshape(EXPERTS * ROWS, width + EXTRA)
    cots = arrived[:, ROWS:, :width].reshape(EXPERTS * COT_ROWS, width)

    slot_in = flat_table.astype(F32)
    slot_scale = lax.rsqrt(jnp.mean(slot_in * slot_in, axis=1, keepdims=True) + EPS)
    slot_cot = jnp.dot(jnp.transpose(selector.astype(BF16)), cotangent, preferred_element_type=F32)
    slot_data = (norm_gain, slot_in, slot_scale, slot_cot)

    acc, note = expert_step(rows, cots, [(own_front, own_rest)] + shards(1))
    note = held_back(rest_ring, note)
    onward(rest_ring)
    acc, note = expert_step(rows, cots, shards(2), (acc, note))
    note = held_back(rest_ring, note)
    last = (rotated(front_ring[-1][0], "split", 1), rotated(rest_ring[-1][1], "split", -1))
    before = expert_step(rows, cots, shards(3), (acc, note))
    partial, local_sums = expert_step(rows, cots, [last], before, slot_data)

    returned = lax.all_to_all(
        partial.reshape(EXPERTS, ROWS, width), "column", split_axis=0, concat_axis=0, tiled=True
    ).reshape(EXPERTS * ROWS, width)
    totals = summed(summed(local_sums, "split"), "column")
    prompt_grads = totals.astype(BF16).reshape(1, TENANTS, PLEN, width)

    home = jnp.arange(EXPERTS * ROWS, dtype=jnp.int32)[None, :]
    f_take = ((f_route * ROWS + CAP + f_rank)[:, None] == home).astype(BF16)
    b_take = ((b_route * ROWS + b_rank)[:, None] == home).astype(BF16)
    f_out = jnp.dot(f_take, returned, preferred_element_type=F32)
    leaving = (fwd_in.astype(F32) + fwd_weights[0] * f_out).astype(BF16)
    next_acts = shifted(leaving, "phase", 1)
    back_out = jnp.dot(b_take, returned, preferred_element_type=F32)
    scaled = bwd_weights[0] * back_out * gain_row[None, :]
    wide = bwd_in.astype(F32)
    inner = jnp.mean(wide * scaled, axis=1, keepdims=True)
    input_grad = cotangent.astype(F32) + bwd_scale * scaled - wide * bwd_scale**3 * inner
    to_prev = jnp.where(bwd_slot[:, None], 0.0, input_grad).astype(BF16)
    prev_grads = shifted(to_prev, "phase", -1)
    return next_acts[None], prev_grads[None], prompt_grads


def solution(mesh):
    names = mesh.axis_names
    phases, experts = mesh.shape[names[0]], mesh.shape[names[1]]
    grid = mesh.devices.reshape(phases, experts // EXPERTS, EXPERTS)
    inner = Mesh(grid, ("phase", "split", "column"))
    both = ("split", "column")
    tokens = P("phase", both, None)
    per_phase = P("phase", None)
    weights = P("phase", both, None, None)
    table = P("phase", None, None, None)
    placed = (
        tokens,
        tokens,
        tokens,
        per_phase,
        per_phase,
        tokens,
        tokens,
        tokens,
        per_phase,
        per_phase,
        tokens,
        table,
        per_phase,
        weights,
        weights,
        weights,
    )
    return jax.shard_map(
        on_device,
        mesh=inner,
        in_specs=placed,
        out_specs=(tokens, tokens, table),
        check_vma=False,
    )
```

```python
import functools

import jax
import jax.numpy as jnp
from jax import lax
from jax.experimental import pallas as pl
from jax.experimental.pallas import tpu as pltpu
from jax.sharding import Mesh, PartitionSpec as P

EXPERTS = 8
TENANTS = 2
PLEN = 10
SLOTS = TENANTS * PLEN
CAP = 18
ROWS = 40
COT_ROWS = 24
BLOCK = ROWS + COT_ROWS
FWD_AT = 16
EXTRA = 128
NO_SLOT = 31
LOW_AT = 32
VMEM_MIB = 24
SHARD_SPACE = pltpu.HBM

EPS = 1e-06
BF16 = jnp.bfloat16
F32 = jnp.float32


def column(row):
    size = row.shape[1]
    down = lax.broadcasted_iota(jnp.int32, (size, size), 0)
    across = lax.broadcasted_iota(jnp.int32, (size, size), 1)
    return jnp.sum(jnp.where(down == across, row, 0.0), axis=1, keepdims=True)


def row_of(col):
    size = col.shape[0]
    down = lax.broadcasted_iota(jnp.int32, (size, size), 0)
    across = lax.broadcasted_iota(jnp.int32, (size, size), 1)
    return jnp.sum(jnp.where(down == across, col, 0.0), axis=0, keepdims=True)


def slots_of(lengths, tenants, token):
    count = lengths.shape[1]
    down = lax.broadcasted_iota(jnp.int32, (count, count), 0)
    across = lax.broadcasted_iota(jnp.int32, (count, count), 1)
    starts = jnp.sum(jnp.where(down < across, column(lengths), 0.0), axis=0, keepdims=True)
    chosen = (starts <= token) & (token < starts + lengths)
    position = token - jnp.sum(jnp.where(chosen, starts, 0.0), axis=1, keepdims=True)
    tenant = jnp.sum(jnp.where(chosen, tenants, 0.0), axis=1, keepdims=True)
    return jnp.where(position < PLEN, tenant * PLEN + position, float(NO_SLOT))


def inputs_of(acts, slot, table):
    lane = lax.broadcasted_iota(jnp.int32, (acts.shape[0], table.shape[0]), 1).astype(F32)
    rows = jnp.dot((lane == slot).astype(BF16), table, preferred_element_type=F32)
    wide = jnp.where(slot < SLOTS, rows, acts.astype(F32))
    scale = lax.rsqrt(jnp.mean(wide * wide, axis=1, keepdims=True) + EPS)
    return wide, scale


def experts_of(routes_row):
    size = routes_row.shape[1]
    down = lax.broadcasted_iota(jnp.int32, (size, size), 0)
    across = lax.broadcasted_iota(jnp.int32, (size, size), 1)
    expert = column(routes_row)
    earlier = (routes_row == expert) & (across < down)
    rank = jnp.sum(jnp.where(earlier, 1.0, 0.0), axis=1, keepdims=True)
    return expert, rank


def prepare_kernel(first_ref, *refs):
    far, refs = refs[:15], refs[15:]
    packed_ref, fin_ref, bin_ref, marks_ref, front_ref, rest_ref, source_ref = refs[:7]
    held, sems, ring_sems = refs[7:-2], refs[-2], refs[-1]
    gate, upper, down = far[12:]
    width, half = gate.shape
    cut = front_ref.shape[0]
    pairs = [
        (gate.at[pl.ds(0, cut), :], front_ref.at[:, pl.ds(0, half)]),
        (upper.at[pl.ds(0, cut), :], front_ref.at[:, pl.ds(half, half)]),
        (gate.at[pl.ds(cut, width - cut), :], rest_ref.at[pl.ds(0, width - cut), pl.ds(0, half)]),
        (upper.at[pl.ds(cut, width - cut), :], rest_ref.at[pl.ds(0, width - cut), pl.ds(half, half)]),
    ]
    for k in range(width // (2 * half)):
        into = rest_ref.at[pl.ds(width - cut + k * half, half), :]
        pairs.append((down.at[:, pl.ds(2 * half * k, 2 * half)], into))
    fetches = [pltpu.make_async_copy(a, b, sems.at[k]) for k, (a, b) in enumerate(zip(far[:12], held))]
    ring_copies = [pltpu.make_async_copy(a, b, ring_sems.at[k]) for k, (a, b) in enumerate(pairs)]
    for copy in fetches + ring_copies:
        copy.start()
    for copy in fetches:
        copy.wait()
    flen_ref, ften_ref, blen_ref, bten_ref, froute_ref, broute_ref, weight_ref, table_ref, gain_ref = held[:9]
    facts_ref, bacts_ref, cot_ref = held[9:]
    tok = facts_ref.shape[0]
    token = lax.broadcasted_iota(jnp.int32, (tok, 1), 0).astype(F32) + first_ref[0, 0].astype(F32)
    table = table_ref[...]
    gain = gain_ref[...]
    f_slot = slots_of(flen_ref[...].astype(F32), ften_ref[...].astype(F32), token)
    b_slot = slots_of(blen_ref[...].astype(F32), bten_ref[...].astype(F32), token)
    f_wide, f_scale = inputs_of(facts_ref[...], f_slot, table)
    b_wide, b_scale = inputs_of(bacts_ref[...], b_slot, table)
    fin_ref[...] = f_wide.astype(BF16)
    bin_ref[...] = b_wide.astype(BF16)
    f_expert, f_rank = experts_of(froute_ref[...].astype(F32))
    b_expert, b_rank = experts_of(broute_ref[...].astype(F32))
    weight = column(weight_ref[...])
    high = weight.astype(BF16).astype(F32)
    lane = lax.broadcasted_iota(jnp.int32, (tok, EXTRA), 1)
    extra = jnp.where(lane == 0, high, jnp.where(lane == 1, weight - high, jnp.where(lane == 2, b_slot, 0.0)))
    blank = jnp.zeros((tok, EXTRA), BF16)
    source_ref[0:tok, 0:width] = (b_wide * b_scale * gain).astype(BF16)
    source_ref[tok : 2 * tok, 0:width] = (f_wide * f_scale * gain).astype(BF16)
    source_ref[2 * tok : 3 * tok, 0:width] = cot_ref[...]
    source_ref[0:tok, width:] = extra.astype(BF16)
    source_ref[tok : 2 * tok, width:] = blank
    source_ref[2 * tok : 3 * tok, width:] = blank
    target = jnp.concatenate(
        [
            row_of(b_expert * BLOCK + b_rank),
            row_of(f_expert * BLOCK + (CAP + f_rank)),
            row_of(b_expert * BLOCK + (ROWS + b_rank)),
        ],
        axis=1,
    )
    total = packed_ref.shape[0]
    place = lax.broadcasted_iota(jnp.int32, (total, 3 * tok), 0).astype(F32)
    picker = (place == target).astype(BF16)
    step = 512
    for at in range(0, width + EXTRA, step):
        cols = slice(at, min(at + step, width + EXTRA))
        packed_ref[:, cols] = jnp.dot(picker, source_ref[:, cols], preferred_element_type=F32).astype(BF16)
    marks_ref[...] = jnp.where(
        lane == 0,
        b_slot,
        jnp.where(
            lane == 1,
            b_scale,
            jnp.where(lane == 2, f_expert * ROWS + (CAP + f_rank), b_expert * ROWS + b_rank),
        ),
    )
    for copy in ring_copies:
        copy.wait()


def prepared(*operands):
    tok, width = operands[10].shape
    half = operands[13].shape[1]
    cut = 3 * width // 4
    near, away = pl.BlockSpec(memory_space=pltpu.VMEM), pl.BlockSpec(memory_space=pl.ANY)
    ring = jax.ShapeDtypeStruct((cut, 2 * half), BF16)
    held = jax.ShapeDtypeStruct((tok, width), BF16)
    return pl.pallas_call(
        prepare_kernel,
        out_shape=(
            jax.ShapeDtypeStruct((EXPERTS * BLOCK, width + EXTRA), BF16),
            held,
            held,
            jax.ShapeDtypeStruct((tok, EXTRA), F32),
            ring,
            ring,
        ),
        in_specs=[pl.BlockSpec(memory_space=pltpu.SMEM)] + [away] * 15,
        out_specs=(near,) * 4 + (away, away),
        scratch_shapes=[pltpu.VMEM((3 * tok, width + EXTRA), BF16)]
        + [pltpu.VMEM(o.shape, o.dtype) for o in operands[1:13]]
        + [pltpu.SemaphoreType.DMA((12,)), pltpu.SemaphoreType.DMA((4 + width // (2 * half),))],
        compiler_params=pltpu.CompilerParams(vmem_limit_bytes=VMEM_MIB * 1024 * 1024),
    )(operands[0], *[pltpu.with_memory_space_constraint(o, pltpu.HBM) for o in operands[1:]])


def expert_kernel(count, has_acc, final, *refs):
    refs = list(refs)
    x_ref, c_ref = refs.pop(0), refs.pop(0)
    sources = [(refs.pop(0), refs.pop(0)) for _ in range(count)]
    acc_ref = None
    if has_acc:
        acc_ref, _ = refs.pop(0), refs.pop(0)
    slot_refs = [refs.pop(0) for _ in range(4)] if final else None
    out_ref, note_ref = refs.pop(0), refs.pop(0)
    gu_ref, down_ref, sems = refs.pop(0), refs.pop(0), refs.pop(0)

    blocks = x_ref.shape[0] // ROWS
    width = c_ref.shape[1]
    step = 512
    contract = (((1,), (1,)), ((), ()))
    row = lax.broadcasted_iota(jnp.int32, (blocks, ROWS - FWD_AT, 1), 1) + FWD_AT
    is_fwd = (row >= CAP) & (row < 2 * CAP)

    fetches = []
    for number, (front, rest) in enumerate(sources):
        cut = front.shape[0]
        group = [
            pltpu.make_async_copy(front, gu_ref.at[number, pl.ds(0, cut), :], sems.at[number, 0]),
            pltpu.make_async_copy(
                rest.at[pl.ds(0, width - cut), :],
                gu_ref.at[number, pl.ds(cut, width - cut), :],
                sems.at[number, 1],
            ),
            pltpu.make_async_copy(
                rest.at[pl.ds(width - cut, down_ref.shape[1]), :], down_ref.at[number], sems.at[number, 2]
            ),
        ]
        fetches.append(group)
        for copy in group:
            copy.start()

    folds = width // gu_ref.shape[2]
    deep = down_ref.shape[1] // folds
    for number, group in enumerate(fetches):
        for copy in group:
            copy.wait()
        down = jnp.concatenate(
            [down_ref[number, k * deep : (k + 1) * deep, :] for k in range(folds)], axis=1
        )
        gu_out = jnp.dot(x_ref[:, :width], gu_ref[number], preferred_element_type=F32)
        half = gu_out.shape[1] // 2
        hidden_grad = lax.dot_general(c_ref[...], down, contract, preferred_element_type=F32)
        gate = gu_out[:, :half].reshape(blocks, ROWS, half)
        upper = gu_out[:, half:].reshape(blocks, ROWS, half)
        gate_f, up_f = gate[:, FWD_AT:], upper[:, FWD_AT:]
        hidden = gate_f / (1.0 + jnp.exp(-gate_f)) * up_f
        hidden = jnp.where(is_fwd, hidden, 0.0)
        hidden = hidden.reshape(blocks * (ROWS - FWD_AT), half).astype(BF16)
        gate_b = gate[:, :COT_ROWS].reshape(blocks * COT_ROWS, half)
        up_b = upper[:, :COT_ROWS].reshape(blocks * COT_ROWS, half)
        sig = 1.0 / (1.0 + jnp.exp(-gate_b))
        gate_grad = hidden_grad * up_b * sig * (1.0 + gate_b * (1.0 - sig))
        up_grad = hidden_grad * (gate_b * sig)
        grads = jnp.concatenate([gate_grad.astype(BF16), up_grad.astype(BF16)], axis=1)
        first = number == 0 and not has_acc
        for n in range(width // step):
            cols = slice(n * step, (n + 1) * step)
            back = lax.dot_general(grads, gu_ref[number, cols, :], contract, preferred_element_type=F32)
            fwd = jnp.dot(hidden, down[:, cols], preferred_element_type=F32)
            back = back.reshape(blocks, COT_ROWS, step)
            fwd = fwd.reshape(blocks, ROWS - FWD_AT, step)
            pieces = [
                back[:, :FWD_AT],
                back[:, FWD_AT:] + fwd[:, : COT_ROWS - FWD_AT],
                fwd[:, COT_ROWS - FWD_AT :],
            ]
            value = jnp.concatenate(pieces, axis=1).reshape(blocks * ROWS, step)
            if not first:
                source = acc_ref if number == 0 else out_ref
                value = value + source[:, cols]
            out_ref[:, cols] = value.astype(out_ref.dtype)

    if final:
        gain_ref, slot_in_ref, scale_ref, cot_ref = slot_refs
        slots = slot_in_ref.shape[0]
        notes = x_ref[:, width:].astype(F32)
        lane = lax.broadcasted_iota(jnp.int32, notes.shape, 1).astype(F32)
        high = jnp.where(lane == notes[:, 2:3], notes[:, 0:1], 0.0)
        low = jnp.where(lane - LOW_AT == notes[:, 2:3], notes[:, 1:2], 0.0)
        weighing = jnp.where(lane < LOW_AT, high, low).astype(BF16)
        both = lax.dot_general(
            weighing, out_ref[...], (((0,), (0,)), ((), ())), preferred_element_type=F32
        )
        slot_q = (both[:slots] + both[LOW_AT : LOW_AT + slots]) * gain_ref[...]
        slot_in = slot_in_ref[...]
        scale = scale_ref[...]
        inner = jnp.mean(slot_in * slot_q, axis=1, keepdims=True)
        note_ref[...] = cot_ref[...] + scale * slot_q - slot_in * (scale * scale * scale * inner)
    else:
        note_ref[...] = jnp.zeros_like(note_ref)


def expert_step(rows, cots, shards, before=None, slot_data=None):
    final = slot_data is not None
    operands = [rows, cots]
    for pair in shards:
        operands += [pltpu.with_memory_space_constraint(part, pltpu.HBM) for part in pair]
    near = pl.BlockSpec(memory_space=pltpu.VMEM)
    specs = [near, near] + [pl.BlockSpec(memory_space=SHARD_SPACE)] * (len(operands) - 2)
    if before is not None:
        operands += list(before)
        specs += [near, near]
    if final:
        operands += list(slot_data)
        specs += [near] * len(slot_data)
    shape = (rows.shape[0], cots.shape[1])
    lanes = shards[0][0].shape[1]
    deep = shards[0][0].shape[0] + shards[0][1].shape[0] - shape[1]
    hidden = len(shards) * lanes // 2
    cost = pl.CostEstimate(
        flops=2 * hidden * shape[1] * (2 * shape[0] + 4 * cots.shape[0]),
        transcendentals=hidden * 2 * cots.shape[0],
        bytes_accessed=sum(o.size * o.dtype.itemsize for o in operands) + 4 * shape[0] * shape[1],
    )
    note = (SLOTS if final else 8, shape[1] if final else 128)
    return pl.pallas_call(
        functools.partial(expert_kernel, len(shards), before is not None, final),
        out_shape=(jax.ShapeDtypeStruct(shape, BF16 if final else F32), jax.ShapeDtypeStruct(note, F32)),
        in_specs=specs,
        out_specs=(near, near),
        scratch_shapes=[
            pltpu.VMEM((len(shards), shape[1], lanes), BF16),
            pltpu.VMEM((len(shards), deep, lanes), BF16),
            pltpu.SemaphoreType.DMA((len(shards), 3)),
        ],
        compiler_params=pltpu.CompilerParams(vmem_limit_bytes=VMEM_MIB * 1024 * 1024),
        cost_estimate=cost,
    )(*operands)


def rotated(value, axis, distance):
    size = lax.axis_size(axis)
    return lax.ppermute(value, axis, [(i, (i + distance) % size) for i in range(size)])


def shifted(block, axis, distance):
    size = lax.axis_size(axis)
    route = [(i, i + distance) for i in range(size) if 0 <= i + distance < size]
    return lax.ppermute(block, axis, route)


def summed(value, axis):
    size = lax.axis_size(axis)
    distance = 1
    while distance < size:
        other = lax.ppermute(value.astype(BF16), axis, [(i, i ^ distance) for i in range(size)])
        value = value.astype(BF16).astype(F32) + other.astype(F32)
        distance *= 2
    return value


def on_device(
    fwd_acts,
    fwd_routes,
    fwd_weights,
    fwd_lengths,
    fwd_tenants,
    bwd_acts,
    bwd_routes,
    bwd_weights,
    bwd_lengths,
    bwd_tenants,
    bwd_cotangent,
    prompts,
    norm_gain,
    w_gate,
    w_up,
    w_down,
):
    tok_count, width = fwd_acts.shape[1:]
    gain_row = norm_gain[0]
    flat_table = prompts[0].reshape(SLOTS, width)

    first_row = (lax.axis_index("split") * lax.axis_size("column") + lax.axis_index("column")) * tok_count
    cotangent = bwd_cotangent[0]
    packed, fwd_in, bwd_in, marks, own_front, own_rest = prepared(
        first_row.astype(jnp.int32).reshape(1, 1),
        fwd_lengths,
        fwd_tenants,
        bwd_lengths,
        bwd_tenants,
        fwd_routes.reshape(1, tok_count),
        bwd_routes.reshape(1, tok_count),
        bwd_weights.reshape(1, tok_count),
        jnp.pad(flat_table, ((0, LOW_AT - SLOTS), (0, 0))),
        norm_gain,
        fwd_acts[0],
        bwd_acts[0],
        cotangent,
        w_gate[0, 0],
        w_up[0, 0],
        w_down[0, 0],
    )
    slot, bwd_scale = marks[:, 0:1], marks[:, 1:2]

    front_ring, rest_ring = [(own_front, own_front)], [(own_rest, own_rest)]

    def onward(ring):
        up, down = ring[-1]
        ring.append((rotated(up, "split", 1), rotated(down, "split", -1)))

    def held_back(ring, note):
        up, down, note = lax.optimization_barrier((*ring[-1], note))
        ring[-1] = (up, down)
        return note

    def shards(step):
        return [(front_ring[step][k], rest_ring[step][k]) for k in range(2)]

    for _ in range(3):
        onward(front_ring)
        onward(rest_ring)

    packed = packed.reshape(EXPERTS, BLOCK, width + EXTRA)
    arrived = lax.all_to_all(packed, "column", split_axis=0, concat_axis=0, tiled=True)
    rows = arrived[:, :ROWS].reshape(EXPERTS * ROWS, width + EXTRA)
    cots = arrived[:, ROWS:, :width].reshape(EXPERTS * COT_ROWS, width)

    slot_in = flat_table.astype(F32)
    slot_scale = lax.rsqrt(jnp.mean(slot_in * slot_in, axis=1, keepdims=True) + EPS)
    selector = (slot == jnp.arange(SLOTS, dtype=F32)[None, :]).astype(BF16)
    slot_cot = jnp.dot(jnp.transpose(selector), cotangent, preferred_element_type=F32)
    slot_data = (norm_gain, slot_in, slot_scale, slot_cot)

    early = [(own_front, own_rest)] + shards(1) + shards(2)
    acc, note = expert_step(rows, cots, early)
    note = held_back(rest_ring, note)
    last = (rotated(front_ring[-1][0], "split", 1), rotated(rest_ring[-1][1], "split", -1))
    before = expert_step(rows, cots, shards(3), (acc, note))
    partial, local_sums = expert_step(rows, cots, [last], before, slot_data)

    returned = lax.all_to_all(
        partial.reshape(EXPERTS, ROWS, width), "column", split_axis=0, concat_axis=0, tiled=True
    ).reshape(EXPERTS * ROWS, width)
    totals = summed(summed(local_sums, "split"), "column")
    prompt_grads = totals.astype(BF16).reshape(1, TENANTS, PLEN, width)

    home = jnp.arange(EXPERTS * ROWS, dtype=jnp.int32).astype(F32)[None, :]
    f_take = (marks[:, 2:3] == home).astype(BF16)
    b_take = (marks[:, 3:4] == home).astype(BF16)
    f_out = jnp.dot(f_take, returned, preferred_element_type=F32)
    leaving = (fwd_in.astype(F32) + fwd_weights[0] * f_out).astype(BF16)
    next_acts = shifted(leaving, "phase", 1)
    back_out = jnp.dot(b_take, returned, preferred_element_type=F32)
    scaled = bwd_weights[0] * back_out * gain_row[None, :]
    wide = bwd_in.astype(F32)
    inner = jnp.mean(wide * scaled, axis=1, keepdims=True)
    input_grad = cotangent.astype(F32) + bwd_scale * scaled - wide * bwd_scale**3 * inner
    to_prev = jnp.where(slot < SLOTS, 0.0, input_grad).astype(BF16)
    prev_grads = shifted(to_prev, "phase", -1)
    return next_acts[None], prev_grads[None], prompt_grads


def solution(mesh):
    names = mesh.axis_names
    phases, experts = mesh.shape[names[0]], mesh.shape[names[1]]
    grid = mesh.devices.reshape(phases, experts // EXPERTS, EXPERTS)
    inner = Mesh(grid, ("phase", "split", "column"))
    both = ("split", "column")
    tokens = P("phase", both, None)
    per_phase = P("phase", None)
    weights = P("phase", both, None, None)
    table = P("phase", None, None, None)
    placed = (
        tokens,
        tokens,
        tokens,
        per_phase,
        per_phase,
        tokens,
        tokens,
        tokens,
        per_phase,
        per_phase,
        tokens,
        table,
        per_phase,
        weights,
        weights,
        weights,
    )
    return jax.shard_map(
        on_device,
        mesh=inner,
        in_specs=placed,
        out_specs=(tokens, tokens, table),
        check_vma=False,
    )
```

```python
import functools

import jax
import jax.numpy as jnp
from jax import lax
from jax.experimental import pallas as pl
from jax.experimental.pallas import tpu as pltpu
from jax.sharding import Mesh, PartitionSpec as P

EXPERTS = 8
TENANTS = 2
PLEN = 10
SLOTS = TENANTS * PLEN
CAP = 18
ROWS = 40
COT_ROWS = 24
BLOCK = ROWS + COT_ROWS
FWD_AT = 16
EXTRA = 128
NO_SLOT = 31
LOW_AT = 32
VMEM_MIB = 24
SHARD_SPACE = pltpu.HBM

EPS = 1e-06
BF16 = jnp.bfloat16
F32 = jnp.float32


def column(row):
    size = row.shape[1]
    down = lax.broadcasted_iota(jnp.int32, (size, size), 0)
    across = lax.broadcasted_iota(jnp.int32, (size, size), 1)
    return jnp.sum(jnp.where(down == across, row, 0.0), axis=1, keepdims=True)


def row_of(col):
    size = col.shape[0]
    down = lax.broadcasted_iota(jnp.int32, (size, size), 0)
    across = lax.broadcasted_iota(jnp.int32, (size, size), 1)
    return jnp.sum(jnp.where(down == across, col, 0.0), axis=0, keepdims=True)


def slots_of(lengths, tenants, token):
    count = lengths.shape[1]
    down = lax.broadcasted_iota(jnp.int32, (count, count), 0)
    across = lax.broadcasted_iota(jnp.int32, (count, count), 1)
    starts = jnp.sum(jnp.where(down < across, column(lengths), 0.0), axis=0, keepdims=True)
    chosen = (starts <= token) & (token < starts + lengths)
    position = token - jnp.sum(jnp.where(chosen, starts, 0.0), axis=1, keepdims=True)
    tenant = jnp.sum(jnp.where(chosen, tenants, 0.0), axis=1, keepdims=True)
    return jnp.where(position < PLEN, tenant * PLEN + position, float(NO_SLOT))


def inputs_of(acts, slot, table):
    lane = lax.broadcasted_iota(jnp.int32, (acts.shape[0], table.shape[0]), 1).astype(F32)
    rows = jnp.dot((lane == slot).astype(BF16), table, preferred_element_type=F32)
    wide = jnp.where(slot < SLOTS, rows, acts.astype(F32))
    scale = lax.rsqrt(jnp.mean(wide * wide, axis=1, keepdims=True) + EPS)
    return wide, scale


def experts_of(routes_row):
    size = routes_row.shape[1]
    down = lax.broadcasted_iota(jnp.int32, (size, size), 0)
    across = lax.broadcasted_iota(jnp.int32, (size, size), 1)
    expert = column(routes_row)
    earlier = (routes_row == expert) & (across < down)
    rank = jnp.sum(jnp.where(earlier, 1.0, 0.0), axis=1, keepdims=True)
    return expert, rank


def prepare_kernel(first_ref, *refs):
    far, refs = refs[:15], refs[15:]
    packed_ref, fin_ref, bin_ref, marks_ref, front_ref, rest_ref, source_ref = refs[:7]
    held, sems, ring_sems = refs[7:-2], refs[-2], refs[-1]
    gate, upper, down = far[12:]
    width, half = gate.shape
    cut = front_ref.shape[0]
    pairs = [
        (gate.at[pl.ds(0, cut), :], front_ref.at[:, pl.ds(0, half)]),
        (upper.at[pl.ds(0, cut), :], front_ref.at[:, pl.ds(half, half)]),
        (gate.at[pl.ds(cut, width - cut), :], rest_ref.at[pl.ds(0, width - cut), pl.ds(0, half)]),
        (upper.at[pl.ds(cut, width - cut), :], rest_ref.at[pl.ds(0, width - cut), pl.ds(half, half)]),
    ]
    for k in range(width // (2 * half)):
        into = rest_ref.at[pl.ds(width - cut + k * half, half), :]
        pairs.append((down.at[:, pl.ds(2 * half * k, 2 * half)], into))
    fetches = [pltpu.make_async_copy(a, b, sems.at[k]) for k, (a, b) in enumerate(zip(far[:12], held))]
    ring_copies = [pltpu.make_async_copy(a, b, ring_sems.at[k]) for k, (a, b) in enumerate(pairs)]
    for copy in fetches + ring_copies:
        copy.start()
    for copy in fetches:
        copy.wait()
    flen_ref, ften_ref, blen_ref, bten_ref, froute_ref, broute_ref, weight_ref, table_ref, gain_ref = held[:9]
    facts_ref, bacts_ref, cot_ref = held[9:]
    tok = facts_ref.shape[0]
    token = lax.broadcasted_iota(jnp.int32, (tok, 1), 0).astype(F32) + first_ref[0, 0].astype(F32)
    table = table_ref[...]
    gain = gain_ref[...]
    f_slot = slots_of(flen_ref[...].astype(F32), ften_ref[...].astype(F32), token)
    b_slot = slots_of(blen_ref[...].astype(F32), bten_ref[...].astype(F32), token)
    f_wide, f_scale = inputs_of(facts_ref[...], f_slot, table)
    b_wide, b_scale = inputs_of(bacts_ref[...], b_slot, table)
    fin_ref[...] = f_wide.astype(BF16)
    bin_ref[...] = b_wide.astype(BF16)
    f_expert, f_rank = experts_of(froute_ref[...].astype(F32))
    b_expert, b_rank = experts_of(broute_ref[...].astype(F32))
    weight = column(weight_ref[...])
    high = weight.astype(BF16).astype(F32)
    lane = lax.broadcasted_iota(jnp.int32, (tok, EXTRA), 1)
    extra = jnp.where(lane == 0, high, jnp.where(lane == 1, weight - high, jnp.where(lane == 2, b_slot, 0.0)))
    blank = jnp.zeros((tok, EXTRA), BF16)
    source_ref[0:tok, 0:width] = (b_wide * b_scale * gain).astype(BF16)
    source_ref[tok : 2 * tok, 0:width] = (f_wide * f_scale * gain).astype(BF16)
    source_ref[2 * tok : 3 * tok, 0:width] = cot_ref[...]
    source_ref[0:tok, width:] = extra.astype(BF16)
    source_ref[tok : 2 * tok, width:] = blank
    source_ref[2 * tok : 3 * tok, width:] = blank
    target = jnp.concatenate(
        [
            row_of(b_expert * BLOCK + b_rank),
            row_of(f_expert * BLOCK + (CAP + f_rank)),
            row_of(b_expert * BLOCK + (ROWS + b_rank)),
        ],
        axis=1,
    )
    total = packed_ref.shape[0]
    place = lax.broadcasted_iota(jnp.int32, (total, 3 * tok), 0).astype(F32)
    picker = (place == target).astype(BF16)
    step = 512
    for at in range(0, width + EXTRA, step):
        cols = slice(at, min(at + step, width + EXTRA))
        packed_ref[:, cols] = jnp.dot(picker, source_ref[:, cols], preferred_element_type=F32).astype(BF16)
    marks_ref[...] = jnp.where(
        lane == 0,
        b_slot,
        jnp.where(
            lane == 1,
            b_scale,
            jnp.where(lane == 2, f_expert * ROWS + (CAP + f_rank), b_expert * ROWS + b_rank),
        ),
    )
    for copy in ring_copies:
        copy.wait()


def prepared(*operands):
    tok, width = operands[10].shape
    half = operands[13].shape[1]
    cut = 3 * width // 4
    near, away = pl.BlockSpec(memory_space=pltpu.VMEM), pl.BlockSpec(memory_space=pl.ANY)
    ring = jax.ShapeDtypeStruct((cut, 2 * half), BF16)
    held = jax.ShapeDtypeStruct((tok, width), BF16)
    return pl.pallas_call(
        prepare_kernel,
        out_shape=(
            jax.ShapeDtypeStruct((EXPERTS * BLOCK, width + EXTRA), BF16),
            held,
            held,
            jax.ShapeDtypeStruct((tok, EXTRA), F32),
            ring,
            ring,
        ),
        in_specs=[pl.BlockSpec(memory_space=pltpu.SMEM)] + [away] * 15,
        out_specs=(near,) * 4 + (away, away),
        scratch_shapes=[pltpu.VMEM((3 * tok, width + EXTRA), BF16)]
        + [pltpu.VMEM(o.shape, o.dtype) for o in operands[1:13]]
        + [pltpu.SemaphoreType.DMA((12,)), pltpu.SemaphoreType.DMA((4 + width // (2 * half),))],
        compiler_params=pltpu.CompilerParams(vmem_limit_bytes=VMEM_MIB * 1024 * 1024),
    )(operands[0], *[pltpu.with_memory_space_constraint(o, pltpu.HBM) for o in operands[1:]])


def slot_weights(notes):
    notes = notes.astype(F32)
    lane = lax.broadcasted_iota(jnp.int32, notes.shape, 1).astype(F32)
    high = jnp.where(lane == notes[:, 2:3], notes[:, 0:1], 0.0)
    low = jnp.where(lane - LOW_AT == notes[:, 2:3], notes[:, 1:2], 0.0)
    return jnp.where(lane < LOW_AT, high, low)


def slot_sums(weighing, values):
    both = lax.dot_general(weighing, values, (((0,), (0,)), ((), ())), preferred_element_type=F32)
    return both[:LOW_AT] + both[LOW_AT : 2 * LOW_AT]


def expert_kernel(count, has_acc, slots, final, *refs):
    refs = list(refs)
    x_ref, c_ref = refs.pop(0), refs.pop(0)
    sources = [(refs.pop(0), refs.pop(0)) for _ in range(count)]
    acc_ref = None
    if has_acc:
        acc_ref, _ = refs.pop(0), refs.pop(0)
    slot_refs = [refs.pop(0) for _ in range(6)] if slots else None
    out_ref, note_ref = refs.pop(0), refs.pop(0)
    gu_ref, down_ref, sems = refs.pop(0), refs.pop(0), refs.pop(0)

    blocks = x_ref.shape[0] // ROWS
    width = c_ref.shape[1]
    step = 512
    contract = (((1,), (1,)), ((), ()))
    row = lax.broadcasted_iota(jnp.int32, (blocks, ROWS - FWD_AT, 1), 1) + FWD_AT
    is_fwd = (row >= CAP) & (row < 2 * CAP)

    fetches = []
    for number, (front, rest) in enumerate(sources):
        cut = front.shape[0]
        group = [
            pltpu.make_async_copy(front, gu_ref.at[number, pl.ds(0, cut), :], sems.at[number, 0]),
            pltpu.make_async_copy(
                rest.at[pl.ds(0, width - cut), :],
                gu_ref.at[number, pl.ds(cut, width - cut), :],
                sems.at[number, 1],
            ),
            pltpu.make_async_copy(
                rest.at[pl.ds(width - cut, down_ref.shape[1]), :], down_ref.at[number], sems.at[number, 2]
            ),
        ]
        fetches.append(group)
        for copy in group:
            copy.start()

    folds = width // gu_ref.shape[2]
    deep = down_ref.shape[1] // folds
    for number, group in enumerate(fetches):
        for copy in group:
            copy.wait()
        if slots and number == count - 1:
            break
        down = jnp.concatenate(
            [down_ref[number, k * deep : (k + 1) * deep, :] for k in range(folds)], axis=1
        )
        gu_out = jnp.dot(x_ref[:, :width], gu_ref[number], preferred_element_type=F32)
        half = gu_out.shape[1] // 2
        hidden_grad = lax.dot_general(c_ref[...], down, contract, preferred_element_type=F32)
        gate = gu_out[:, :half].reshape(blocks, ROWS, half)
        upper = gu_out[:, half:].reshape(blocks, ROWS, half)
        gate_f, up_f = gate[:, FWD_AT:], upper[:, FWD_AT:]
        hidden = gate_f / (1.0 + jnp.exp(-gate_f)) * up_f
        hidden = jnp.where(is_fwd, hidden, 0.0)
        hidden = hidden.reshape(blocks * (ROWS - FWD_AT), half).astype(BF16)
        gate_b = gate[:, :COT_ROWS].reshape(blocks * COT_ROWS, half)
        up_b = upper[:, :COT_ROWS].reshape(blocks * COT_ROWS, half)
        sig = 1.0 / (1.0 + jnp.exp(-gate_b))
        gate_grad = hidden_grad * up_b * sig * (1.0 + gate_b * (1.0 - sig))
        up_grad = hidden_grad * (gate_b * sig)
        grads = jnp.concatenate([gate_grad.astype(BF16), up_grad.astype(BF16)], axis=1)
        first = number == 0 and not has_acc
        for n in range(width // step):
            cols = slice(n * step, (n + 1) * step)
            back = lax.dot_general(grads, gu_ref[number, cols, :], contract, preferred_element_type=F32)
            fwd = jnp.dot(hidden, down[:, cols], preferred_element_type=F32)
            back = back.reshape(blocks, COT_ROWS, step)
            fwd = fwd.reshape(blocks, ROWS - FWD_AT, step)
            pieces = [
                back[:, :FWD_AT],
                back[:, FWD_AT:] + fwd[:, : COT_ROWS - FWD_AT],
                fwd[:, COT_ROWS - FWD_AT :],
            ]
            value = jnp.concatenate(pieces, axis=1).reshape(blocks * ROWS, step)
            if not first:
                source = acc_ref if number == 0 else out_ref
                value = value + source[:, cols]
            out_ref[:, cols] = value.astype(out_ref.dtype)

    if slots:
        gain_ref, slot_in_ref, scale_ref, slot_cot_ref, normed_ref, far_ref = slot_refs
        number = count - 1
        down = jnp.concatenate(
            [down_ref[number, k * deep : (k + 1) * deep, :] for k in range(folds)], axis=1
        )
        gu_out = jnp.dot(normed_ref[...], gu_ref[number], preferred_element_type=F32)
        half = gu_out.shape[1] // 2
        gate, upper = gu_out[:, :half], gu_out[:, half:]
        hidden_grad = lax.dot_general(far_ref[...], down, contract, preferred_element_type=F32)
        sig = 1.0 / (1.0 + jnp.exp(-gate))
        gate_grad = hidden_grad * upper * sig * (1.0 + gate * (1.0 - sig))
        up_grad = hidden_grad * (gate * sig)
        grads = jnp.concatenate([gate_grad.astype(BF16), up_grad.astype(BF16)], axis=1)
        far = lax.dot_general(grads, gu_ref[number], contract, preferred_element_type=F32)
        weighing = slot_weights(x_ref[:, width:]).astype(BF16)
        slot_q = (slot_sums(weighing, out_ref[...].astype(BF16)) + far)[:SLOTS] * gain_ref[...]
        slot_in = slot_in_ref[...]
        scale = scale_ref[...]
        inner = jnp.mean(slot_in * slot_q, axis=1, keepdims=True)
        note_ref[...] = slot_cot_ref[...] + scale * slot_q - slot_in * (scale * scale * scale * inner)
    elif final:
        note_ref[...] = jnp.zeros_like(note_ref)
    elif not has_acc:
        weighing = slot_weights(x_ref[:, width:]).reshape(blocks, ROWS, EXTRA)[:, :COT_ROWS]
        weighing = weighing.reshape(blocks * COT_ROWS, EXTRA).astype(BF16)
        note_ref[...] = slot_sums(weighing, c_ref[...]).astype(note_ref.dtype)


def expert_step(rows, cots, shards, before=None, slot_data=(), final=False):
    slots = bool(slot_data)
    operands = [rows, cots]
    for pair in shards:
        operands += [pltpu.with_memory_space_constraint(part, pltpu.HBM) for part in pair]
    near = pl.BlockSpec(memory_space=pltpu.VMEM)
    specs = [near, near] + [pl.BlockSpec(memory_space=SHARD_SPACE)] * (len(operands) - 2)
    if before is not None:
        operands += list(before)
        specs += [near, near]
    operands += list(slot_data)
    specs += [near] * len(slot_data)
    shape = (rows.shape[0], cots.shape[1])
    lanes = shards[0][0].shape[1]
    deep = shards[0][0].shape[0] + shards[0][1].shape[0] - shape[1]
    hidden = len(shards) * lanes // 2
    cost = pl.CostEstimate(
        flops=2 * hidden * shape[1] * (2 * shape[0] + 4 * cots.shape[0]),
        transcendentals=hidden * 2 * cots.shape[0],
        bytes_accessed=sum(o.size * o.dtype.itemsize for o in operands) + 4 * shape[0] * shape[1],
    )
    if slots:
        note = jax.ShapeDtypeStruct((SLOTS, shape[1]), F32)
    elif final:
        note = jax.ShapeDtypeStruct((8, 128), F32)
    else:
        note = jax.ShapeDtypeStruct((LOW_AT, shape[1]), BF16)
    return pl.pallas_call(
        functools.partial(expert_kernel, len(shards), before is not None, slots, final),
        out_shape=(jax.ShapeDtypeStruct(shape, BF16 if final else F32), note),
        in_specs=specs,
        out_specs=(near, near),
        scratch_shapes=[
            pltpu.VMEM((len(shards), shape[1], lanes), BF16),
            pltpu.VMEM((len(shards), deep, lanes), BF16),
            pltpu.SemaphoreType.DMA((len(shards), 3)),
        ],
        compiler_params=pltpu.CompilerParams(vmem_limit_bytes=VMEM_MIB * 1024 * 1024),
        cost_estimate=cost,
    )(*operands)


def rotated(value, axis, distance):
    size = lax.axis_size(axis)
    return lax.ppermute(value, axis, [(i, (i + distance) % size) for i in range(size)])


def shifted(block, axis, distance):
    size = lax.axis_size(axis)
    route = [(i, i + distance) for i in range(size) if 0 <= i + distance < size]
    return lax.ppermute(block, axis, route)


def summed(value, axis):
    size = lax.axis_size(axis)
    distance = 1
    while distance < size:
        other = lax.ppermute(value.astype(BF16), axis, [(i, i ^ distance) for i in range(size)])
        value = value.astype(BF16).astype(F32) + other.astype(F32)
        distance *= 2
    return value


def on_device(
    fwd_acts,
    fwd_routes,
    fwd_weights,
    fwd_lengths,
    fwd_tenants,
    bwd_acts,
    bwd_routes,
    bwd_weights,
    bwd_lengths,
    bwd_tenants,
    bwd_cotangent,
    prompts,
    norm_gain,
    w_gate,
    w_up,
    w_down,
):
    tok_count, width = fwd_acts.shape[1:]
    gain_row = norm_gain[0]
    flat_table = prompts[0].reshape(SLOTS, width)

    first_row = (lax.axis_index("split") * lax.axis_size("column") + lax.axis_index("column")) * tok_count
    cotangent = bwd_cotangent[0]
    packed, fwd_in, bwd_in, marks, own_front, own_rest = prepared(
        first_row.astype(jnp.int32).reshape(1, 1),
        fwd_lengths,
        fwd_tenants,
        bwd_lengths,
        bwd_tenants,
        fwd_routes.reshape(1, tok_count),
        bwd_routes.reshape(1, tok_count),
        bwd_weights.reshape(1, tok_count),
        jnp.pad(flat_table, ((0, LOW_AT - SLOTS), (0, 0))),
        norm_gain,
        fwd_acts[0],
        bwd_acts[0],
        cotangent,
        w_gate[0, 0],
        w_up[0, 0],
        w_down[0, 0],
    )
    slot, bwd_scale = marks[:, 0:1], marks[:, 1:2]

    front_ring, rest_ring = [(own_front, own_front)], [(own_rest, own_rest)]

    def onward(ring):
        up, down = ring[-1]
        ring.append((rotated(up, "split", 1), rotated(down, "split", -1)))

    def held_back(ring, note):
        up, down, note = lax.optimization_barrier((*ring[-1], note))
        ring[-1] = (up, down)
        return note

    def shards(step):
        return [(front_ring[step][k], rest_ring[step][k]) for k in range(2)]

    for _ in range(3):
        onward(front_ring)
        onward(rest_ring)

    packed = packed.reshape(EXPERTS, BLOCK, width + EXTRA)
    arrived = lax.all_to_all(packed, "column", split_axis=0, concat_axis=0, tiled=True)
    rows = arrived[:, :ROWS].reshape(EXPERTS * ROWS, width + EXTRA)
    cots = arrived[:, ROWS:, :width].reshape(EXPERTS * COT_ROWS, width)

    slot_in = flat_table.astype(F32)
    slot_scale = lax.rsqrt(jnp.mean(slot_in * slot_in, axis=1, keepdims=True) + EPS)
    selector = (slot == jnp.arange(SLOTS, dtype=F32)[None, :]).astype(BF16)
    slot_cot = jnp.dot(jnp.transpose(selector), cotangent, preferred_element_type=F32)
    slot_normed = jnp.pad((slot_in * slot_scale * norm_gain).astype(BF16), ((0, LOW_AT - SLOTS), (0, 0)))

    early = [(own_front, own_rest)] + shards(1) + shards(2)
    acc, note = expert_step(rows, cots, early)
    far_sums = rotated(note, "split", lax.axis_size("split") // 2)
    note = held_back(rest_ring, note)
    last = (rotated(front_ring[-1][0], "split", 1), rotated(rest_ring[-1][1], "split", -1))
    slot_data = (norm_gain, slot_in, slot_scale, slot_cot, slot_normed, far_sums)
    acc, local_sums = expert_step(rows, cots, shards(3) + [(own_front, own_rest)], (acc, note), slot_data)
    partial, _ = expert_step(rows, cots, [last], (acc, local_sums), final=True)

    returned = lax.all_to_all(
        partial.reshape(EXPERTS, ROWS, width), "column", split_axis=0, concat_axis=0, tiled=True
    ).reshape(EXPERTS * ROWS, width)
    totals = summed(summed(local_sums, "split"), "column")
    prompt_grads = totals.astype(BF16).reshape(1, TENANTS, PLEN, width)

    home = jnp.arange(EXPERTS * ROWS, dtype=jnp.int32).astype(F32)[None, :]
    f_take = (marks[:, 2:3] == home).astype(BF16)
    b_take = (marks[:, 3:4] == home).astype(BF16)
    f_out = jnp.dot(f_take, returned, preferred_element_type=F32)
    leaving = (fwd_in.astype(F32) + fwd_weights[0] * f_out).astype(BF16)
    next_acts = shifted(leaving, "phase", 1)
    back_out = jnp.dot(b_take, returned, preferred_element_type=F32)
    scaled = bwd_weights[0] * back_out * gain_row[None, :]
    wide = bwd_in.astype(F32)
    inner = jnp.mean(wide * scaled, axis=1, keepdims=True)
    input_grad = cotangent.astype(F32) + bwd_scale * scaled - wide * bwd_scale**3 * inner
    to_prev = jnp.where(slot < SLOTS, 0.0, input_grad).astype(BF16)
    prev_grads = shifted(to_prev, "phase", -1)
    return next_acts[None], prev_grads[None], prompt_grads


def solution(mesh):
    names = mesh.axis_names
    phases, experts = mesh.shape[names[0]], mesh.shape[names[1]]
    grid = mesh.devices.reshape(phases, experts // EXPERTS, EXPERTS)
    inner = Mesh(grid, ("phase", "split", "column"))
    both = ("split", "column")
    tokens = P("phase", both, None)
    per_phase = P("phase", None)
    weights = P("phase", both, None, None)
    table = P("phase", None, None, None)
    placed = (
        tokens,
        tokens,
        tokens,
        per_phase,
        per_phase,
        tokens,
        tokens,
        tokens,
        per_phase,
        per_phase,
        tokens,
        table,
        per_phase,
        weights,
        weights,
        weights,
    )
    return jax.shard_map(
        on_device,
        mesh=inner,
        in_specs=placed,
        out_specs=(tokens, tokens, table),
        check_vma=False,
    )
```

```python
import functools

import jax
import jax.numpy as jnp
from jax import lax
from jax.experimental import pallas as pl
from jax.experimental.pallas import tpu as pltpu
from jax.sharding import Mesh, PartitionSpec as P

EXPERTS = 8
TENANTS = 2
PLEN = 10
SLOTS = TENANTS * PLEN
CAP = 18
ROWS = 40
COT_ROWS = 24
BLOCK = ROWS + COT_ROWS
FWD_AT = 16
EXTRA = 128
NO_SLOT = 31
LOW_AT = 32
VMEM_MIB = 24
SHARD_SPACE = pltpu.HBM

EPS = 1e-06
BF16 = jnp.bfloat16
F32 = jnp.float32


def column(row):
    size = row.shape[1]
    down = lax.broadcasted_iota(jnp.int32, (size, size), 0)
    across = lax.broadcasted_iota(jnp.int32, (size, size), 1)
    return jnp.sum(jnp.where(down == across, row, 0.0), axis=1, keepdims=True)


def row_of(col):
    size = col.shape[0]
    down = lax.broadcasted_iota(jnp.int32, (size, size), 0)
    across = lax.broadcasted_iota(jnp.int32, (size, size), 1)
    return jnp.sum(jnp.where(down == across, col, 0.0), axis=0, keepdims=True)


def slots_of(lengths, tenants, token):
    count = lengths.shape[1]
    down = lax.broadcasted_iota(jnp.int32, (count, count), 0)
    across = lax.broadcasted_iota(jnp.int32, (count, count), 1)
    starts = jnp.sum(jnp.where(down < across, column(lengths), 0.0), axis=0, keepdims=True)
    chosen = (starts <= token) & (token < starts + lengths)
    position = token - jnp.sum(jnp.where(chosen, starts, 0.0), axis=1, keepdims=True)
    tenant = jnp.sum(jnp.where(chosen, tenants, 0.0), axis=1, keepdims=True)
    return jnp.where(position < PLEN, tenant * PLEN + position, float(NO_SLOT))


def inputs_of(acts, slot, table):
    lane = lax.broadcasted_iota(jnp.int32, (acts.shape[0], table.shape[0]), 1).astype(F32)
    rows = jnp.dot((lane == slot).astype(BF16), table, preferred_element_type=F32)
    wide = jnp.where(slot < SLOTS, rows, acts.astype(F32))
    scale = lax.rsqrt(jnp.mean(wide * wide, axis=1, keepdims=True) + EPS)
    return wide, scale


def experts_of(routes_row):
    size = routes_row.shape[1]
    down = lax.broadcasted_iota(jnp.int32, (size, size), 0)
    across = lax.broadcasted_iota(jnp.int32, (size, size), 1)
    expert = column(routes_row)
    earlier = (routes_row == expert) & (across < down)
    rank = jnp.sum(jnp.where(earlier, 1.0, 0.0), axis=1, keepdims=True)
    return expert, rank


def prepare_kernel(first_ref, *refs):
    far, refs = refs[:15], refs[15:]
    packed_ref, fin_ref, bin_ref, marks_ref, front_ref, rest_ref, source_ref = refs[:7]
    held, sems, ring_sems = refs[7:-2], refs[-2], refs[-1]
    gate, upper, down = far[12:]
    width, half = gate.shape
    cut = front_ref.shape[0]
    pairs = [
        (gate.at[pl.ds(0, cut), :], front_ref.at[:, pl.ds(0, half)]),
        (upper.at[pl.ds(0, cut), :], front_ref.at[:, pl.ds(half, half)]),
        (gate.at[pl.ds(cut, width - cut), :], rest_ref.at[pl.ds(0, width - cut), pl.ds(0, half)]),
        (upper.at[pl.ds(cut, width - cut), :], rest_ref.at[pl.ds(0, width - cut), pl.ds(half, half)]),
    ]
    for k in range(width // (2 * half)):
        into = rest_ref.at[pl.ds(width - cut + k * half, half), :]
        pairs.append((down.at[:, pl.ds(2 * half * k, 2 * half)], into))
    fetches = [pltpu.make_async_copy(a, b, sems.at[k]) for k, (a, b) in enumerate(zip(far[:12], held))]
    ring_copies = [pltpu.make_async_copy(a, b, ring_sems.at[k]) for k, (a, b) in enumerate(pairs)]
    for copy in fetches + ring_copies:
        copy.start()
    for copy in fetches:
        copy.wait()
    flen_ref, ften_ref, blen_ref, bten_ref, froute_ref, broute_ref, weight_ref, table_ref, gain_ref = held[:9]
    facts_ref, bacts_ref, cot_ref = held[9:]
    tok = facts_ref.shape[0]
    token = lax.broadcasted_iota(jnp.int32, (tok, 1), 0).astype(F32) + first_ref[0, 0].astype(F32)
    table = table_ref[...]
    gain = gain_ref[...]
    f_slot = slots_of(flen_ref[...].astype(F32), ften_ref[...].astype(F32), token)
    b_slot = slots_of(blen_ref[...].astype(F32), bten_ref[...].astype(F32), token)
    f_wide, f_scale = inputs_of(facts_ref[...], f_slot, table)
    b_wide, b_scale = inputs_of(bacts_ref[...], b_slot, table)
    fin_ref[...] = f_wide.astype(BF16)
    bin_ref[...] = b_wide.astype(BF16)
    f_expert, f_rank = experts_of(froute_ref[...].astype(F32))
    b_expert, b_rank = experts_of(broute_ref[...].astype(F32))
    weight = column(weight_ref[...])
    high = weight.astype(BF16).astype(F32)
    lane = lax.broadcasted_iota(jnp.int32, (tok, EXTRA), 1)
    extra = jnp.where(lane == 0, high, jnp.where(lane == 1, weight - high, jnp.where(lane == 2, b_slot, 0.0)))
    blank = jnp.zeros((tok, EXTRA), BF16)
    source_ref[0:tok, 0:width] = (b_wide * b_scale * gain).astype(BF16)
    source_ref[tok : 2 * tok, 0:width] = (f_wide * f_scale * gain).astype(BF16)
    source_ref[2 * tok : 3 * tok, 0:width] = cot_ref[...]
    source_ref[0:tok, width:] = extra.astype(BF16)
    source_ref[tok : 2 * tok, width:] = blank
    source_ref[2 * tok : 3 * tok, width:] = blank
    target = jnp.concatenate(
        [
            row_of(b_expert * BLOCK + b_rank),
            row_of(f_expert * BLOCK + (CAP + f_rank)),
            row_of(b_expert * BLOCK + (ROWS + b_rank)),
        ],
        axis=1,
    )
    total = packed_ref.shape[0]
    place = lax.broadcasted_iota(jnp.int32, (total, 3 * tok), 0).astype(F32)
    picker = (place == target).astype(BF16)
    step = 512
    for at in range(0, width + EXTRA, step):
        cols = slice(at, min(at + step, width + EXTRA))
        packed_ref[:, cols] = jnp.dot(picker, source_ref[:, cols], preferred_element_type=F32).astype(BF16)
    marks_ref[...] = jnp.where(
        lane == 0,
        b_slot,
        jnp.where(
            lane == 1,
            b_scale,
            jnp.where(lane == 2, f_expert * ROWS + (CAP + f_rank), b_expert * ROWS + b_rank),
        ),
    )
    for copy in ring_copies:
        copy.wait()


def prepared(*operands):
    tok, width = operands[10].shape
    half = operands[13].shape[1]
    cut = 3 * width // 4
    near, away = pl.BlockSpec(memory_space=pltpu.VMEM), pl.BlockSpec(memory_space=pl.ANY)
    ring = jax.ShapeDtypeStruct((cut, 2 * half), BF16)
    held = jax.ShapeDtypeStruct((tok, width), BF16)
    return pl.pallas_call(
        prepare_kernel,
        out_shape=(
            jax.ShapeDtypeStruct((EXPERTS * BLOCK, width + EXTRA), BF16),
            held,
            held,
            jax.ShapeDtypeStruct((tok, EXTRA), F32),
            ring,
            ring,
        ),
        in_specs=[pl.BlockSpec(memory_space=pltpu.SMEM)] + [away] * 15,
        out_specs=(near,) * 4 + (away, away),
        scratch_shapes=[pltpu.VMEM((3 * tok, width + EXTRA), BF16)]
        + [pltpu.VMEM(o.shape, o.dtype) for o in operands[1:13]]
        + [pltpu.SemaphoreType.DMA((12,)), pltpu.SemaphoreType.DMA((4 + width // (2 * half),))],
        compiler_params=pltpu.CompilerParams(vmem_limit_bytes=VMEM_MIB * 1024 * 1024),
    )(operands[0], *[pltpu.with_memory_space_constraint(o, pltpu.HBM) for o in operands[1:]])


def expert_kernel(count, has_acc, final, *refs):
    refs = list(refs)
    x_ref, c_ref = refs.pop(0), refs.pop(0)
    sources = [(refs.pop(0), refs.pop(0)) for _ in range(count)]
    acc_ref = None
    if has_acc:
        acc_ref, _ = refs.pop(0), refs.pop(0)
    slot_refs = [refs.pop(0) for _ in range(4)] if final else None
    out_ref, note_ref = refs.pop(0), refs.pop(0)
    gu_ref, down_ref, sems = refs.pop(0), refs.pop(0), refs.pop(0)

    blocks = x_ref.shape[0] // ROWS
    width = c_ref.shape[1]
    step = 512
    contract = (((1,), (1,)), ((), ()))
    row = lax.broadcasted_iota(jnp.int32, (blocks, ROWS - FWD_AT, 1), 1) + FWD_AT
    is_fwd = (row >= CAP) & (row < 2 * CAP)

    fetches = []
    for number, (front, rest) in enumerate(sources):
        cut = front.shape[0]
        group = [
            pltpu.make_async_copy(front, gu_ref.at[number, pl.ds(0, cut), :], sems.at[number, 0]),
            pltpu.make_async_copy(
                rest.at[pl.ds(0, width - cut), :],
                gu_ref.at[number, pl.ds(cut, width - cut), :],
                sems.at[number, 1],
            ),
            pltpu.make_async_copy(
                rest.at[pl.ds(width - cut, down_ref.shape[1]), :], down_ref.at[number], sems.at[number, 2]
            ),
        ]
        fetches.append(group)
        for copy in group:
            copy.start()

    folds = width // gu_ref.shape[2]
    deep = down_ref.shape[1] // folds
    for number, group in enumerate(fetches):
        for copy in group:
            copy.wait()
        down = jnp.concatenate(
            [down_ref[number, k * deep : (k + 1) * deep, :] for k in range(folds)], axis=1
        )
        gu_out = jnp.dot(x_ref[:, :width], gu_ref[number], preferred_element_type=F32)
        half = gu_out.shape[1] // 2
        hidden_grad = lax.dot_general(c_ref[...], down, contract, preferred_element_type=F32)
        gate = gu_out[:, :half].reshape(blocks, ROWS, half)
        upper = gu_out[:, half:].reshape(blocks, ROWS, half)
        gate_f, up_f = gate[:, FWD_AT:], upper[:, FWD_AT:]
        hidden = gate_f / (1.0 + jnp.exp(-gate_f)) * up_f
        hidden = jnp.where(is_fwd, hidden, 0.0)
        hidden = hidden.reshape(blocks * (ROWS - FWD_AT), half).astype(BF16)
        gate_b = gate[:, :COT_ROWS].reshape(blocks * COT_ROWS, half)
        up_b = upper[:, :COT_ROWS].reshape(blocks * COT_ROWS, half)
        sig = 1.0 / (1.0 + jnp.exp(-gate_b))
        gate_grad = hidden_grad * up_b * sig * (1.0 + gate_b * (1.0 - sig))
        up_grad = hidden_grad * (gate_b * sig)
        grads = jnp.concatenate([gate_grad.astype(BF16), up_grad.astype(BF16)], axis=1)
        first = number == 0 and not has_acc
        for n in range(width // step):
            cols = slice(n * step, (n + 1) * step)
            back = lax.dot_general(grads, gu_ref[number, cols, :], contract, preferred_element_type=F32)
            fwd = jnp.dot(hidden, down[:, cols], preferred_element_type=F32)
            back = back.reshape(blocks, COT_ROWS, step)
            fwd = fwd.reshape(blocks, ROWS - FWD_AT, step)
            pieces = [
                back[:, :FWD_AT],
                back[:, FWD_AT:] + fwd[:, : COT_ROWS - FWD_AT],
                fwd[:, COT_ROWS - FWD_AT :],
            ]
            value = jnp.concatenate(pieces, axis=1).reshape(blocks * ROWS, step)
            if not first:
                source = acc_ref if number == 0 else out_ref
                value = value + source[:, cols]
            out_ref[:, cols] = value.astype(out_ref.dtype)

    if final:
        gain_ref, slot_in_ref, scale_ref, cot_ref = slot_refs
        slots = slot_in_ref.shape[0]
        notes = x_ref[:, width:].astype(F32)
        lane = lax.broadcasted_iota(jnp.int32, notes.shape, 1).astype(F32)
        high = jnp.where(lane == notes[:, 2:3], notes[:, 0:1], 0.0)
        low = jnp.where(lane - LOW_AT == notes[:, 2:3], notes[:, 1:2], 0.0)
        weighing = jnp.where(lane < LOW_AT, high, low).astype(BF16)
        both = lax.dot_general(
            weighing, out_ref[...], (((0,), (0,)), ((), ())), preferred_element_type=F32
        )
        slot_q = (both[:slots] + both[LOW_AT : LOW_AT + slots]) * gain_ref[...]
        slot_in = slot_in_ref[...]
        scale = scale_ref[...]
        inner = jnp.mean(slot_in * slot_q, axis=1, keepdims=True)
        note_ref[...] = cot_ref[...] + scale * slot_q - slot_in * (scale * scale * scale * inner)
    else:
        note_ref[...] = jnp.zeros_like(note_ref)


def expert_step(rows, cots, shards, before=None, slot_data=None):
    final = slot_data is not None
    operands = [rows, cots]
    for pair in shards:
        operands += [pltpu.with_memory_space_constraint(part, pltpu.HBM) for part in pair]
    near = pl.BlockSpec(memory_space=pltpu.VMEM)
    specs = [near, near] + [pl.BlockSpec(memory_space=SHARD_SPACE)] * (len(operands) - 2)
    if before is not None:
        operands += list(before)
        specs += [near, near]
    if final:
        operands += list(slot_data)
        specs += [near] * len(slot_data)
    shape = (rows.shape[0], cots.shape[1])
    lanes = shards[0][0].shape[1]
    deep = shards[0][0].shape[0] + shards[0][1].shape[0] - shape[1]
    hidden = len(shards) * lanes // 2
    cost = pl.CostEstimate(
        flops=2 * hidden * shape[1] * (2 * shape[0] + 4 * cots.shape[0]),
        transcendentals=hidden * 2 * cots.shape[0],
        bytes_accessed=sum(o.size * o.dtype.itemsize for o in operands) + 4 * shape[0] * shape[1],
    )
    note = (SLOTS if final else 8, shape[1] if final else 128)
    return pl.pallas_call(
        functools.partial(expert_kernel, len(shards), before is not None, final),
        out_shape=(jax.ShapeDtypeStruct(shape, BF16 if final else F32), jax.ShapeDtypeStruct(note, F32)),
        in_specs=specs,
        out_specs=(near, near),
        scratch_shapes=[
            pltpu.VMEM((len(shards), shape[1], lanes), BF16),
            pltpu.VMEM((len(shards), deep, lanes), BF16),
            pltpu.SemaphoreType.DMA((len(shards), 3)),
        ],
        compiler_params=pltpu.CompilerParams(vmem_limit_bytes=VMEM_MIB * 1024 * 1024),
        cost_estimate=cost,
    )(*operands)


def rotated(value, axis, distance):
    size = lax.axis_size(axis)
    return lax.ppermute(value, axis, [(i, (i + distance) % size) for i in range(size)])


def shifted(block, axis, distance):
    size = lax.axis_size(axis)
    route = [(i, i + distance) for i in range(size) if 0 <= i + distance < size]
    return lax.ppermute(block, axis, route)


def summed(value, axis):
    size = lax.axis_size(axis)
    distance = 1
    while distance < size:
        other = lax.ppermute(value.astype(BF16), axis, [(i, i ^ distance) for i in range(size)])
        value = value.astype(BF16).astype(F32) + other.astype(F32)
        distance *= 2
    return value


def on_device(
    fwd_acts,
    fwd_routes,
    fwd_weights,
    fwd_lengths,
    fwd_tenants,
    bwd_acts,
    bwd_routes,
    bwd_weights,
    bwd_lengths,
    bwd_tenants,
    bwd_cotangent,
    prompts,
    norm_gain,
    w_gate,
    w_up,
    w_down,
):
    tok_count, width = fwd_acts.shape[1:]
    gain_row = norm_gain[0]
    flat_table = prompts[0].reshape(SLOTS, width)

    first_row = (lax.axis_index("split") * lax.axis_size("column") + lax.axis_index("column")) * tok_count
    cotangent = bwd_cotangent[0]
    packed, fwd_in, bwd_in, marks, own_front, own_rest = prepared(
        first_row.astype(jnp.int32).reshape(1, 1),
        fwd_lengths,
        fwd_tenants,
        bwd_lengths,
        bwd_tenants,
        fwd_routes.reshape(1, tok_count),
        bwd_routes.reshape(1, tok_count),
        bwd_weights.reshape(1, tok_count),
        jnp.pad(flat_table, ((0, LOW_AT - SLOTS), (0, 0))),
        norm_gain,
        fwd_acts[0],
        bwd_acts[0],
        cotangent,
        w_gate[0, 0],
        w_up[0, 0],
        w_down[0, 0],
    )
    slot, bwd_scale = marks[:, 0:1], marks[:, 1:2]

    front_ring, rest_ring = [(own_front, own_front)], [(own_rest, own_rest)]

    def onward(ring):
        up, down = ring[-1]
        ring.append((rotated(up, "split", 1), rotated(down, "split", -1)))

    def shards(step):
        return [(front_ring[step][k], rest_ring[step][k]) for k in range(2)]

    for _ in range(3):
        onward(front_ring)
        onward(rest_ring)

    packed = packed.reshape(EXPERTS, BLOCK, width + EXTRA)
    arrived = lax.all_to_all(packed, "column", split_axis=0, concat_axis=0, tiled=True)
    rows = arrived[:, :ROWS].reshape(EXPERTS * ROWS, width + EXTRA)
    cots = arrived[:, ROWS:, :width].reshape(EXPERTS * COT_ROWS, width)

    slot_in = flat_table.astype(F32)
    slot_scale = lax.rsqrt(jnp.mean(slot_in * slot_in, axis=1, keepdims=True) + EPS)
    selector = (slot == jnp.arange(SLOTS, dtype=F32)[None, :]).astype(BF16)
    slot_cot = jnp.dot(jnp.transpose(selector), cotangent, preferred_element_type=F32)
    slot_data = (norm_gain, slot_in, slot_scale, slot_cot)

    early = [(own_front, own_rest)] + shards(1) + shards(2)
    acc, note = expert_step(rows, cots, early)
    last = (rotated(front_ring[-1][0], "split", 1), rotated(rest_ring[-1][1], "split", -1))
    before = expert_step(rows, cots, shards(3), (acc, note))
    partial, local_sums = expert_step(rows, cots, [last], before, slot_data)

    returned = lax.all_to_all(
        partial.reshape(EXPERTS, ROWS, width), "column", split_axis=0, concat_axis=0, tiled=True
    ).reshape(EXPERTS * ROWS, width)
    totals = summed(summed(local_sums, "split"), "column")
    prompt_grads = totals.astype(BF16).reshape(1, TENANTS, PLEN, width)

    home = jnp.arange(EXPERTS * ROWS, dtype=jnp.int32).astype(F32)[None, :]
    f_take = (marks[:, 2:3] == home).astype(BF16)
    b_take = (marks[:, 3:4] == home).astype(BF16)
    f_out = jnp.dot(f_take, returned, preferred_element_type=F32)
    leaving = (fwd_in.astype(F32) + fwd_weights[0] * f_out).astype(BF16)
    next_acts = shifted(leaving, "phase", 1)
    back_out = jnp.dot(b_take, returned, preferred_element_type=F32)
    scaled = bwd_weights[0] * back_out * gain_row[None, :]
    wide = bwd_in.astype(F32)
    inner = jnp.mean(wide * scaled, axis=1, keepdims=True)
    input_grad = cotangent.astype(F32) + bwd_scale * scaled - wide * bwd_scale**3 * inner
    to_prev = jnp.where(slot < SLOTS, 0.0, input_grad).astype(BF16)
    prev_grads = shifted(to_prev, "phase", -1)
    return next_acts[None], prev_grads[None], prompt_grads


def solution(mesh):
    names = mesh.axis_names
    phases, experts = mesh.shape[names[0]], mesh.shape[names[1]]
    grid = mesh.devices.reshape(phases, experts // EXPERTS, EXPERTS)
    inner = Mesh(grid, ("phase", "split", "column"))
    both = ("split", "column")
    tokens = P("phase", both, None)
    per_phase = P("phase", None)
    weights = P("phase", both, None, None)
    table = P("phase", None, None, None)
    placed = (
        tokens,
        tokens,
        tokens,
        per_phase,
        per_phase,
        tokens,
        tokens,
        tokens,
        per_phase,
        per_phase,
        tokens,
        table,
        per_phase,
        weights,
        weights,
        weights,
    )
    return jax.shard_map(
        on_device,
        mesh=inner,
        in_specs=placed,
        out_specs=(tokens, tokens, table),
        check_vma=False,
    )
```

```python
import functools

import jax
import jax.numpy as jnp
from jax import lax
from jax.experimental import pallas as pl
from jax.experimental.pallas import tpu as pltpu
from jax.sharding import Mesh, PartitionSpec as P

EXPERTS = 8
TENANTS = 2
PLEN = 10
SLOTS = TENANTS * PLEN
CAP = 18
ROWS = 40
COT_ROWS = 24
BLOCK = ROWS + COT_ROWS
FWD_AT = 16
EXTRA = 128
NO_SLOT = 31
LOW_AT = 32
VMEM_MIB = 24
SHARD_SPACE = pltpu.HBM

EPS = 1e-06
BF16 = jnp.bfloat16
F32 = jnp.float32


def column(row):
    size = row.shape[1]
    down = lax.broadcasted_iota(jnp.int32, (size, size), 0)
    across = lax.broadcasted_iota(jnp.int32, (size, size), 1)
    return jnp.sum(jnp.where(down == across, row, 0.0), axis=1, keepdims=True)


def row_of(col):
    size = col.shape[0]
    down = lax.broadcasted_iota(jnp.int32, (size, size), 0)
    across = lax.broadcasted_iota(jnp.int32, (size, size), 1)
    return jnp.sum(jnp.where(down == across, col, 0.0), axis=0, keepdims=True)


def slots_of(lengths, tenants, token):
    count = lengths.shape[1]
    down = lax.broadcasted_iota(jnp.int32, (count, count), 0)
    across = lax.broadcasted_iota(jnp.int32, (count, count), 1)
    starts = jnp.sum(jnp.where(down < across, column(lengths), 0.0), axis=0, keepdims=True)
    chosen = (starts <= token) & (token < starts + lengths)
    position = token - jnp.sum(jnp.where(chosen, starts, 0.0), axis=1, keepdims=True)
    tenant = jnp.sum(jnp.where(chosen, tenants, 0.0), axis=1, keepdims=True)
    return jnp.where(position < PLEN, tenant * PLEN + position, float(NO_SLOT))


def inputs_of(acts, slot, table):
    lane = lax.broadcasted_iota(jnp.int32, (acts.shape[0], table.shape[0]), 1).astype(F32)
    rows = jnp.dot((lane == slot).astype(BF16), table, preferred_element_type=F32)
    wide = jnp.where(slot < SLOTS, rows, acts.astype(F32))
    scale = lax.rsqrt(jnp.mean(wide * wide, axis=1, keepdims=True) + EPS)
    return wide, scale


def experts_of(routes_row):
    size = routes_row.shape[1]
    down = lax.broadcasted_iota(jnp.int32, (size, size), 0)
    across = lax.broadcasted_iota(jnp.int32, (size, size), 1)
    expert = column(routes_row)
    earlier = (routes_row == expert) & (across < down)
    rank = jnp.sum(jnp.where(earlier, 1.0, 0.0), axis=1, keepdims=True)
    return expert, rank


def prepare_kernel(first_ref, *refs):
    far, refs = refs[:15], refs[15:]
    packed_ref, fin_ref, bin_ref, marks_ref, front_ref, rest_ref, source_ref = refs[:7]
    held, sems, ring_sems = refs[7:-2], refs[-2], refs[-1]
    gate, upper, down = far[12:]
    width, half = gate.shape
    cut = front_ref.shape[0]
    pairs = [
        (gate.at[pl.ds(0, cut), :], front_ref.at[:, pl.ds(0, half)]),
        (upper.at[pl.ds(0, cut), :], front_ref.at[:, pl.ds(half, half)]),
        (gate.at[pl.ds(cut, width - cut), :], rest_ref.at[pl.ds(0, width - cut), pl.ds(0, half)]),
        (upper.at[pl.ds(cut, width - cut), :], rest_ref.at[pl.ds(0, width - cut), pl.ds(half, half)]),
    ]
    for k in range(width // (2 * half)):
        into = rest_ref.at[pl.ds(width - cut + k * half, half), :]
        pairs.append((down.at[:, pl.ds(2 * half * k, 2 * half)], into))
    fetches = [pltpu.make_async_copy(a, b, sems.at[k]) for k, (a, b) in enumerate(zip(far[:12], held))]
    ring_copies = [pltpu.make_async_copy(a, b, ring_sems.at[k]) for k, (a, b) in enumerate(pairs)]
    for copy in fetches + ring_copies:
        copy.start()
    for copy in fetches:
        copy.wait()
    flen_ref, ften_ref, blen_ref, bten_ref, froute_ref, broute_ref, weight_ref, table_ref, gain_ref = held[:9]
    facts_ref, bacts_ref, cot_ref = held[9:]
    tok = facts_ref.shape[0]
    token = lax.broadcasted_iota(jnp.int32, (tok, 1), 0).astype(F32) + first_ref[0, 0].astype(F32)
    table = table_ref[...]
    gain = gain_ref[...]
    f_slot = slots_of(flen_ref[...].astype(F32), ften_ref[...].astype(F32), token)
    b_slot = slots_of(blen_ref[...].astype(F32), bten_ref[...].astype(F32), token)
    f_wide, f_scale = inputs_of(facts_ref[...], f_slot, table)
    b_wide, b_scale = inputs_of(bacts_ref[...], b_slot, table)
    fin_ref[...] = f_wide.astype(BF16)
    bin_ref[...] = b_wide.astype(BF16)
    f_expert, f_rank = experts_of(froute_ref[...].astype(F32))
    b_expert, b_rank = experts_of(broute_ref[...].astype(F32))
    weight = column(weight_ref[...])
    high = weight.astype(BF16).astype(F32)
    lane = lax.broadcasted_iota(jnp.int32, (tok, EXTRA), 1)
    extra = jnp.where(lane == 0, high, jnp.where(lane == 1, weight - high, jnp.where(lane == 2, b_slot, 0.0)))
    blank = jnp.zeros((tok, EXTRA), BF16)
    source_ref[0:tok, 0:width] = (b_wide * b_scale * gain).astype(BF16)
    source_ref[tok : 2 * tok, 0:width] = (f_wide * f_scale * gain).astype(BF16)
    source_ref[2 * tok : 3 * tok, 0:width] = cot_ref[...]
    source_ref[0:tok, width:] = extra.astype(BF16)
    source_ref[tok : 2 * tok, width:] = blank
    source_ref[2 * tok : 3 * tok, width:] = blank
    target = jnp.concatenate(
        [
            row_of(b_expert * BLOCK + b_rank),
            row_of(f_expert * BLOCK + (CAP + f_rank)),
            row_of(b_expert * BLOCK + (ROWS + b_rank)),
        ],
        axis=1,
    )
    total = packed_ref.shape[0]
    place = lax.broadcasted_iota(jnp.int32, (total, 3 * tok), 0).astype(F32)
    picker = (place == target).astype(BF16)
    step = 512
    for at in range(0, width + EXTRA, step):
        cols = slice(at, min(at + step, width + EXTRA))
        packed_ref[:, cols] = jnp.dot(picker, source_ref[:, cols], preferred_element_type=F32).astype(BF16)
    marks_ref[...] = jnp.where(
        lane == 0,
        b_slot,
        jnp.where(
            lane == 1,
            b_scale,
            jnp.where(lane == 2, f_expert * ROWS + (CAP + f_rank), b_expert * ROWS + b_rank),
        ),
    )
    for copy in ring_copies:
        copy.wait()


def prepared(*operands):
    tok, width = operands[10].shape
    half = operands[13].shape[1]
    cut = 3 * width // 4
    near, away = pl.BlockSpec(memory_space=pltpu.VMEM), pl.BlockSpec(memory_space=pl.ANY)
    ring = jax.ShapeDtypeStruct((cut, 2 * half), BF16)
    held = jax.ShapeDtypeStruct((tok, width), BF16)
    return pl.pallas_call(
        prepare_kernel,
        out_shape=(
            jax.ShapeDtypeStruct((EXPERTS * BLOCK, width + EXTRA), BF16),
            held,
            held,
            jax.ShapeDtypeStruct((tok, EXTRA), F32),
            ring,
            ring,
        ),
        in_specs=[pl.BlockSpec(memory_space=pltpu.SMEM)] + [away] * 15,
        out_specs=(near,) * 4 + (away, away),
        scratch_shapes=[pltpu.VMEM((3 * tok, width + EXTRA), BF16)]
        + [pltpu.VMEM(o.shape, o.dtype) for o in operands[1:13]]
        + [pltpu.SemaphoreType.DMA((12,)), pltpu.SemaphoreType.DMA((4 + width // (2 * half),))],
        compiler_params=pltpu.CompilerParams(vmem_limit_bytes=VMEM_MIB * 1024 * 1024),
    )(operands[0], *[pltpu.with_memory_space_constraint(o, pltpu.HBM) for o in operands[1:]])


def expert_kernel(count, has_acc, final, *refs):
    refs = list(refs)
    x_ref, c_ref = refs.pop(0), refs.pop(0)
    sources = [(refs.pop(0), refs.pop(0)) for _ in range(count)]
    acc_ref = None
    if has_acc:
        acc_ref, _ = refs.pop(0), refs.pop(0)
    slot_refs = [refs.pop(0) for _ in range(4)] if final else None
    out_ref, note_ref = refs.pop(0), refs.pop(0)
    gu_ref, down_ref, sems = refs.pop(0), refs.pop(0), refs.pop(0)

    blocks = x_ref.shape[0] // ROWS
    width = c_ref.shape[1]
    step = 512
    contract = (((1,), (1,)), ((), ()))
    row = lax.broadcasted_iota(jnp.int32, (blocks, ROWS - FWD_AT, 1), 1) + FWD_AT
    is_fwd = (row >= CAP) & (row < 2 * CAP)

    fetches = []
    for number, (front, rest) in enumerate(sources):
        cut = front.shape[0]
        group = [
            pltpu.make_async_copy(front, gu_ref.at[number, pl.ds(0, cut), :], sems.at[number, 0]),
            pltpu.make_async_copy(
                rest.at[pl.ds(0, width - cut), :],
                gu_ref.at[number, pl.ds(cut, width - cut), :],
                sems.at[number, 1],
            ),
            pltpu.make_async_copy(
                rest.at[pl.ds(width - cut, down_ref.shape[1]), :], down_ref.at[number], sems.at[number, 2]
            ),
        ]
        fetches.append(group)
        for copy in group:
            copy.start()

    folds = width // gu_ref.shape[2]
    deep = down_ref.shape[1] // folds
    for number, group in enumerate(fetches):
        for copy in group:
            copy.wait()
        down = jnp.concatenate(
            [down_ref[number, k * deep : (k + 1) * deep, :] for k in range(folds)], axis=1
        )
        gu_out = jnp.dot(x_ref[:, :width], gu_ref[number], preferred_element_type=F32)
        half = gu_out.shape[1] // 2
        hidden_grad = lax.dot_general(c_ref[...], down, contract, preferred_element_type=F32)
        gate = gu_out[:, :half].reshape(blocks, ROWS, half)
        upper = gu_out[:, half:].reshape(blocks, ROWS, half)
        gate_f, up_f = gate[:, FWD_AT:], upper[:, FWD_AT:]
        hidden = gate_f / (1.0 + jnp.exp(-gate_f)) * up_f
        hidden = jnp.where(is_fwd, hidden, 0.0)
        hidden = hidden.reshape(blocks * (ROWS - FWD_AT), half).astype(BF16)
        gate_b = gate[:, :COT_ROWS].reshape(blocks * COT_ROWS, half)
        up_b = upper[:, :COT_ROWS].reshape(blocks * COT_ROWS, half)
        sig = 1.0 / (1.0 + jnp.exp(-gate_b))
        gate_grad = hidden_grad * up_b * sig * (1.0 + gate_b * (1.0 - sig))
        up_grad = hidden_grad * (gate_b * sig)
        grads = jnp.concatenate([gate_grad.astype(BF16), up_grad.astype(BF16)], axis=1)
        first = number == 0 and not has_acc
        for n in range(width // step):
            cols = slice(n * step, (n + 1) * step)
            back = lax.dot_general(grads, gu_ref[number, cols, :], contract, preferred_element_type=F32)
            fwd = jnp.dot(hidden, down[:, cols], preferred_element_type=F32)
            back = back.reshape(blocks, COT_ROWS, step)
            fwd = fwd.reshape(blocks, ROWS - FWD_AT, step)
            pieces = [
                back[:, :FWD_AT],
                back[:, FWD_AT:] + fwd[:, : COT_ROWS - FWD_AT],
                fwd[:, COT_ROWS - FWD_AT :],
            ]
            value = jnp.concatenate(pieces, axis=1).reshape(blocks * ROWS, step)
            if not first:
                source = acc_ref if number == 0 else out_ref
                value = value + source[:, cols]
            out_ref[:, cols] = value.astype(out_ref.dtype)

    if final:
        gain_ref, slot_in_ref, scale_ref, cot_ref = slot_refs
        slots = slot_in_ref.shape[0]
        notes = x_ref[:, width:].astype(F32)
        lane = lax.broadcasted_iota(jnp.int32, notes.shape, 1).astype(F32)
        high = jnp.where(lane == notes[:, 2:3], notes[:, 0:1], 0.0)
        low = jnp.where(lane - LOW_AT == notes[:, 2:3], notes[:, 1:2], 0.0)
        weighing = jnp.where(lane < LOW_AT, high, low).astype(BF16)
        both = lax.dot_general(
            weighing, out_ref[...], (((0,), (0,)), ((), ())), preferred_element_type=F32
        )
        slot_q = (both[:slots] + both[LOW_AT : LOW_AT + slots]) * gain_ref[...]
        slot_in = slot_in_ref[...]
        scale = scale_ref[...]
        inner = jnp.mean(slot_in * slot_q, axis=1, keepdims=True)
        note_ref[...] = cot_ref[...] + scale * slot_q - slot_in * (scale * scale * scale * inner)
    else:
        note_ref[...] = jnp.zeros_like(note_ref)


def expert_step(rows, cots, shards, before=None, slot_data=None):
    final = slot_data is not None
    operands = [rows, cots]
    for pair in shards:
        operands += [pltpu.with_memory_space_constraint(part, pltpu.HBM) for part in pair]
    near = pl.BlockSpec(memory_space=pltpu.VMEM)
    specs = [near, near] + [pl.BlockSpec(memory_space=SHARD_SPACE)] * (len(operands) - 2)
    if before is not None:
        operands += list(before)
        specs += [near, near]
    if final:
        operands += list(slot_data)
        specs += [near] * len(slot_data)
    shape = (rows.shape[0], cots.shape[1])
    lanes = shards[0][0].shape[1]
    deep = shards[0][0].shape[0] + shards[0][1].shape[0] - shape[1]
    hidden = len(shards) * lanes // 2
    cost = pl.CostEstimate(
        flops=2 * hidden * shape[1] * (2 * shape[0] + 4 * cots.shape[0]),
        transcendentals=hidden * 2 * cots.shape[0],
        bytes_accessed=sum(o.size * o.dtype.itemsize for o in operands) + 4 * shape[0] * shape[1],
    )
    note = (SLOTS if final else 8, shape[1] if final else 128)
    return pl.pallas_call(
        functools.partial(expert_kernel, len(shards), before is not None, final),
        out_shape=(jax.ShapeDtypeStruct(shape, BF16 if final else F32), jax.ShapeDtypeStruct(note, F32)),
        in_specs=specs,
        out_specs=(near, near),
        scratch_shapes=[
            pltpu.VMEM((len(shards), shape[1], lanes), BF16),
            pltpu.VMEM((len(shards), deep, lanes), BF16),
            pltpu.SemaphoreType.DMA((len(shards), 3)),
        ],
        compiler_params=pltpu.CompilerParams(vmem_limit_bytes=VMEM_MIB * 1024 * 1024),
        cost_estimate=cost,
    )(*operands)


def rotated(value, axis, distance):
    size = lax.axis_size(axis)
    return lax.ppermute(value, axis, [(i, (i + distance) % size) for i in range(size)])


def shifted(block, axis, distance):
    size = lax.axis_size(axis)
    route = [(i, i + distance) for i in range(size) if 0 <= i + distance < size]
    return lax.ppermute(block, axis, route)


def summed(value, axis):
    size = lax.axis_size(axis)
    distance = size // 2
    while distance:
        other = lax.ppermute(value.astype(BF16), axis, [(i, i ^ distance) for i in range(size)])
        value = value.astype(BF16).astype(F32) + other.astype(F32)
        distance //= 2
    return value


def on_device(
    fwd_acts,
    fwd_routes,
    fwd_weights,
    fwd_lengths,
    fwd_tenants,
    bwd_acts,
    bwd_routes,
    bwd_weights,
    bwd_lengths,
    bwd_tenants,
    bwd_cotangent,
    prompts,
    norm_gain,
    w_gate,
    w_up,
    w_down,
):
    tok_count, width = fwd_acts.shape[1:]
    gain_row = norm_gain[0]
    flat_table = prompts[0].reshape(SLOTS, width)

    first_row = (lax.axis_index("split") * lax.axis_size("column") + lax.axis_index("column")) * tok_count
    cotangent = bwd_cotangent[0]
    packed, fwd_in, bwd_in, marks, own_front, own_rest = prepared(
        first_row.astype(jnp.int32).reshape(1, 1),
        fwd_lengths,
        fwd_tenants,
        bwd_lengths,
        bwd_tenants,
        fwd_routes.reshape(1, tok_count),
        bwd_routes.reshape(1, tok_count),
        bwd_weights.reshape(1, tok_count),
        jnp.pad(flat_table, ((0, LOW_AT - SLOTS), (0, 0))),
        norm_gain,
        fwd_acts[0],
        bwd_acts[0],
        cotangent,
        w_gate[0, 0],
        w_up[0, 0],
        w_down[0, 0],
    )
    slot, bwd_scale = marks[:, 0:1], marks[:, 1:2]

    front_ring, rest_ring = [(own_front, own_front)], [(own_rest, own_rest)]

    def onward(ring):
        up, down = ring[-1]
        ring.append((rotated(up, "split", 1), rotated(down, "split", -1)))

    def shards(step):
        return [(front_ring[step][k], rest_ring[step][k]) for k in range(2)]

    for _ in range(3):
        onward(front_ring)
        onward(rest_ring)

    packed = packed.reshape(EXPERTS, BLOCK, width + EXTRA)
    arrived = lax.all_to_all(packed, "column", split_axis=0, concat_axis=0, tiled=True)
    rows = arrived[:, :ROWS].reshape(EXPERTS * ROWS, width + EXTRA)
    cots = arrived[:, ROWS:, :width].reshape(EXPERTS * COT_ROWS, width)

    slot_in = flat_table.astype(F32)
    slot_scale = lax.rsqrt(jnp.mean(slot_in * slot_in, axis=1, keepdims=True) + EPS)
    selector = (slot == jnp.arange(SLOTS, dtype=F32)[None, :]).astype(BF16)
    slot_cot = jnp.dot(jnp.transpose(selector), cotangent, preferred_element_type=F32)
    slot_data = (norm_gain, slot_in, slot_scale, slot_cot)

    early = [(own_front, own_rest)] + shards(1) + shards(2)
    acc, note = expert_step(rows, cots, early)
    last = (rotated(front_ring[-1][0], "split", 1), rotated(rest_ring[-1][1], "split", -1))
    before = expert_step(rows, cots, shards(3), (acc, note))
    partial, local_sums = expert_step(rows, cots, [last], before, slot_data)

    returned = lax.all_to_all(
        partial.reshape(EXPERTS, ROWS, width), "column", split_axis=0, concat_axis=0, tiled=True
    ).reshape(EXPERTS * ROWS, width)
    totals = summed(summed(local_sums, "split"), "column")
    prompt_grads = totals.astype(BF16).reshape(1, TENANTS, PLEN, width)

    home = jnp.arange(EXPERTS * ROWS, dtype=jnp.int32).astype(F32)[None, :]
    f_take = (marks[:, 2:3] == home).astype(BF16)
    b_take = (marks[:, 3:4] == home).astype(BF16)
    f_out = jnp.dot(f_take, returned, preferred_element_type=F32)
    leaving = (fwd_in.astype(F32) + fwd_weights[0] * f_out).astype(BF16)
    next_acts = shifted(leaving, "phase", 1)
    back_out = jnp.dot(b_take, returned, preferred_element_type=F32)
    scaled = bwd_weights[0] * back_out * gain_row[None, :]
    wide = bwd_in.astype(F32)
    inner = jnp.mean(wide * scaled, axis=1, keepdims=True)
    input_grad = cotangent.astype(F32) + bwd_scale * scaled - wide * bwd_scale**3 * inner
    to_prev = jnp.where(slot < SLOTS, 0.0, input_grad).astype(BF16)
    prev_grads = shifted(to_prev, "phase", -1)
    return next_acts[None], prev_grads[None], prompt_grads


def solution(mesh):
    names = mesh.axis_names
    phases, experts = mesh.shape[names[0]], mesh.shape[names[1]]
    grid = mesh.devices.reshape(phases, experts // EXPERTS, EXPERTS)
    inner = Mesh(grid, ("phase", "split", "column"))
    both = ("split", "column")
    tokens = P("phase", both, None)
    per_phase = P("phase", None)
    weights = P("phase", both, None, None)
    table = P("phase", None, None, None)
    placed = (
        tokens,
        tokens,
        tokens,
        per_phase,
        per_phase,
        tokens,
        tokens,
        tokens,
        per_phase,
        per_phase,
        tokens,
        table,
        per_phase,
        weights,
        weights,
        weights,
    )
    return jax.shard_map(
        on_device,
        mesh=inner,
        in_specs=placed,
        out_specs=(tokens, tokens, table),
        check_vma=False,
    )
```
